32 devices in a mesh: dp: 4 (over y, core), row: 2 (over x), col: 4 (over z).
Axes of the slice: x: 2, y: 2, z: 4, core: 2. Of those that a mesh axis runs over, the one named last changes fastest.
Arguments:
- tokens: bfloat16 [12288, 768], P(('dp', 'col'), 'row'), may hold values from -6 to 6
- cotangent: bfloat16 [12288, 768], P(('dp', 'col'), 'row'), may hold values from -6 to 6
- timestep: int32 [4], P('dp'), may hold values from 0 to 999
- piece_starts: int32 [4, 4], P('dp'), may hold values from 0 to 2816, as said below
- w_mod: bfloat16 [128, 6, 768], P(None, None, 'row'), may hold values from -0.5 to 0.5
- b_mod: float32 [6, 768], P(None, 'row'), may hold values from -3 to 3
- gain_attn: float32 [768], P('row'), may hold values from 0.5 to 1.5
- w_qkv: bfloat16 [2304, 768], P('col', 'row'), may hold values from -0.21875 to 0.21875
- w_out: bfloat16 [768, 768], P('col', 'row'), may hold values from -0.875 to 0.875
- gain_mlp: float32 [768], P('row'), may hold values from 0.5 to 1.5
- w_up: bfloat16 [768, 3072], P('row', 'col'), may hold values from -0.21875 to 0.21875
- b_up: bfloat16 [3072], P('col'), may hold values from -3 to 3
- w_down: bfloat16 [3072, 768], P('col', 'row'), may hold values from -0.109375 to 0.109375
- b_down: float32 [768], P('row'), may hold values from -3 to 3
Outputs:
- block_out: bfloat16 [12288, 768], P(('dp', 'col'), 'row')
- d_tokens: float32 [12288, 768], P(('dp', 'col'), 'row')
- d_mod_w: float32 [128, 6, 768], P(None, None, 'row')
- d_mod_b: float32 [6, 768], P(None, 'row')
- d_gain_attn: float32 [768], P('row')
- d_qkv: float32 [2304, 768], P('col', 'row')
- d_out_proj: float32 [768, 768], P('col', 'row')
- d_gain_mlp: float32 [768], P('row')
- d_up: float32 [768, 3072], P('row', 'col')
- d_up_bias: float32 [3072], P('col')
- d_down: float32 [3072, 768], P('col', 'row')
- d_down_bias: float32 [768], P('row')
The draws below stay inside these ranges and needn't reach their ends.
Inputs may be any that keep to these rules, and one draw needn't show every extreme that they name: `piece_starts`: in every sequence the 4 pieces of 256 tokens rise, do not intersect and lie inside the sequence; the first opens the sequence and the last closes it.
All inputs are finite; a program needn't handle non-finite values.
Results may differ from the reference program's by a relative error of at most 0.014.
The reference program's roundings to bfloat16 on the way count: a program that leaves them out, or rounds other values in their place, can miss the bound.
Values may be sent and summed in bfloat16 or wider, within the bound.
No kernel may reach another device: no remote copies, remote signals or barrier semaphores. Data moves between devices by JAX's collectives and lax.ppermute only.
A program may use at most 192 MiB of HBM per device.

```python
import math
import jax
import jax.numpy as jnp
from jax import lax

D = 768
HEADS = 12
HEAD = 64
FF = 3072
COND = 128
SEQ_LEN = 3072
PIECE = 256
PIECES = 4
SEQS = 4
TOKENS = 12288


def draw_piece_starts(key, part):
    region = SEQ_LEN // PIECES
    offsets = jax.random.randint(key, (SEQS, PIECES), 0, region - PIECE + 1)
    column = jnp.arange(PIECES, dtype=jnp.int32)[None, :]
    offsets = jnp.where(column == 0, 0, offsets)
    offsets = jnp.where(column == PIECES - 1, region - PIECE, offsets)
    return (column * region + offsets).astype(jnp.int32)


def touch_ends(result, key, least, high):
    longest = result.shape.index(max(result.shape))
    spots = []
    for shift in (0, 1):
        where = [jax.random.randint(jax.random.fold_in(key, axis), (), 0, length) for axis, length in enumerate(result.shape)]
        where[longest] = (where[longest] + shift) % result.shape[longest]
        spots.append(tuple(where))
    return result.at[spots[0]].set(least).at[spots[1]].set(high)


def level_of(stream_key, shape, split, low, largest):
    loudness = 1.0
    for dim, blocks in split:
        heights = jax.random.uniform(jax.random.fold_in(jax.random.fold_in(stream_key, 6), dim), (blocks,), jnp.float32, low / len(split), largest / len(split))
        loudness = loudness * jnp.repeat(jnp.exp(heights), shape[dim] // blocks).reshape((-1,) + (1,) * (len(shape) - 1 - dim))
    return loudness


def bell_draw(key, extent, spread, bound, cuts=(), kind=jnp.bfloat16):
    gain = level_of(key, extent, cuts, -0.22, 0.18) if cuts else 1.0
    drawn = jax.random.normal(key, extent, jnp.float32) * spread * gain
    return jnp.minimum(jnp.maximum(drawn, -bound), bound).astype(kind)


def setup_inputs(seed: int = 0) -> dict:
    arg_keys = jax.random.split(jax.random.key(seed), 15)
    tokens = bell_draw(arg_keys[0], (TOKENS, D), 1.0, 6.0, ((0, 16), (1, 2)))
    cotangent = bell_draw(arg_keys[1], (TOKENS, D), 1.0, 6.0, ((0, 16), (1, 2)))
    timestep = touch_ends(jax.random.randint(arg_keys[2], (SEQS,), 0, 1000), jax.random.fold_in(arg_keys[2], 1), 0, 999).astype(jnp.int32)
    piece_starts = draw_piece_starts(jax.random.fold_in(arg_keys[14], 71), 0)
    w_mod = bell_draw(arg_keys[4], (COND, 6, D), COND ** -0.5, 0.5, ((2, 2),))
    b_mod = bell_draw(arg_keys[5], (6, D), 0.5, 3.0, ((1, 2),), jnp.float32)
    gain_attn = jnp.clip(1.0 + 0.1 * jax.random.normal(arg_keys[6], (D,), jnp.float32), 0.5, 1.5)
    w_qkv = bell_draw(arg_keys[7], (3 * D, D), D ** -0.5, 0.21875, ((0, 4), (1, 2)))
    w_out = bell_draw(arg_keys[8], (D, D), (D // 16) ** -0.5, 0.875, ((0, 4), (1, 2)))
    gain_mlp = jnp.clip(1.0 + 0.1 * jax.random.normal(arg_keys[9], (D,), jnp.float32), 0.5, 1.5)
    w_up = bell_draw(arg_keys[10], (D, FF), D ** -0.5, 0.21875, ((0, 2), (1, 4)))
    b_up = bell_draw(arg_keys[11], (FF,), 0.5, 3.0, ((0, 4),))
    w_down = bell_draw(arg_keys[12], (FF, D), FF ** -0.5, 0.109375, ((0, 4), (1, 2)))
    b_down = bell_draw(arg_keys[13], (D,), 0.5, 3.0, ((0, 2),), jnp.float32)
    return dict(tokens=tokens, cotangent=cotangent, timestep=timestep, piece_starts=piece_starts, w_mod=w_mod, b_mod=b_mod, gain_attn=gain_attn, w_qkv=w_qkv, w_out=w_out, gain_mlp=gain_mlp, w_up=w_up, b_up=b_up, w_down=w_down, b_down=b_down)


precise = lax.Precision.HIGHEST
epsilon = 1e-05

@jax.custom_vjp
def low(v):
    return lax.optimization_barrier(v.astype(jnp.bfloat16)).astype(jnp.float32)

@jax.custom_vjp
def low_back(v):
    return v

def low_keep(v):
    return (low(v), None)

def low_pass(kept, grad):
    return (grad,)

def back_keep(v):
    return (v, None)

def back_low(kept, grad):
    return (low(grad),)
low.defvjp(low_keep, low_pass)
low_back.defvjp(back_keep, back_low)

def embed_time(time_step):
    half_size = COND // 2
    frequency = jnp.exp(-math.log(10000.0) * jnp.arange(half_size, dtype=jnp.float32) / half_size)
    angles = time_step * frequency
    return jax.nn.silu(jnp.concatenate([jnp.cos(angles), jnp.sin(angles)]))

def rotate(vectors, places):
    half_size = HEAD // 2
    frequency = jnp.exp(-math.log(10000.0) * jnp.arange(half_size, dtype=jnp.float32) / half_size)
    angles = places.astype(jnp.float32)[:, None] * frequency[None, :]
    cosine = jnp.cos(angles)[:, None, :]
    sine_part = jnp.sin(angles)[:, None, :]
    first_half = vectors[..., :half_size]
    second_half = vectors[..., half_size:]
    return jnp.concatenate([first_half * cosine - second_half * sine_part, second_half * cosine + first_half * sine_part], -1)

def piece_ids(places, starts):
    inside = (places[:, None] >= starts[None, :]) & (places[:, None] < starts[None, :] + PIECE)
    labels = jnp.arange(1, PIECES + 1, dtype=jnp.int32)[None, :]
    return lax.optimization_barrier(jnp.sum(jnp.where(inside, labels, 0), axis=1)).astype(jnp.int32) - 1

def layer_norm(values, gain_vec):
    row_mean = lax.optimization_barrier(jnp.mean(values, -1, keepdims=True))
    centered = values - row_mean
    variance = lax.optimization_barrier(jnp.mean(centered * centered, -1, keepdims=True))
    return centered * lax.rsqrt(variance + epsilon) * gain_vec

def one_sequence(residual, starts, time_step, params):
    w_mod, b_mod, gain_attn, w_qkv, w_out, gain_mlp, w_up, b_up, w_down, b_down = params
    condition = embed_time(time_step)
    modulation = jnp.einsum('k,kjd->jd', condition, w_mod, precision=precise) + b_mod
    normed_in = low(layer_norm(residual, gain_attn) * (1.0 + modulation[1]) + modulation[0])
    projected = low_back(jnp.dot(normed_in, w_qkv.T, precision=precise)).reshape(SEQ_LEN, HEADS, 3, HEAD)
    places = jnp.arange(SEQ_LEN, dtype=jnp.int32)
    queries = low(rotate(projected[:, :, 0], places))
    keys_rot = low(rotate(projected[:, :, 1], places))
    values_part = low(projected[:, :, 2])
    pieces = piece_ids(places, starts)
    allowed = (places[None, :] <= places[:, None]) | (pieces[:, None] == pieces[None, :]) & (pieces[:, None] >= 0)

    def one_head(operands):
        query_head, key_head, value_head = operands
        scores = low_back(jnp.dot(query_head, key_head.T, precision=precise) * HEAD ** (-0.5))
        scores = jnp.where(allowed, scores, -1e+30)
        probabilities = low(jax.nn.softmax(scores, axis=-1))
        return jnp.dot(probabilities, value_head, precision=precise)
    mixed = lax.map(jax.checkpoint(one_head), (queries.transpose(1, 0, 2), keys_rot.transpose(1, 0, 2), values_part.transpose(1, 0, 2)))
    mixed = low_back(low(mixed.transpose(1, 0, 2).reshape(SEQ_LEN, D)))
    attended = low_back(jnp.dot(mixed, w_out, precision=precise))
    middle = residual + modulation[2] * attended
    normed_mid = low(layer_norm(middle, gain_mlp) * (1.0 + modulation[4]) + modulation[3])
    hidden = low_back(jnp.dot(normed_mid, w_up, precision=precise) + b_up)
    active = low(jax.nn.gelu(hidden, approximate=True))
    branch = low_back(jnp.dot(active, w_down, precision=precise) + b_down)
    return middle + modulation[5] * branch

def reference(tokens, cotangent, timestep, piece_starts, w_mod, b_mod, gain_attn, w_qkv, w_out, gain_mlp, w_up, b_up, w_down, b_down):
    params = tuple((p.astype(jnp.float32) for p in (w_mod, b_mod, gain_attn, w_qkv, w_out, gain_mlp, w_up, b_up, w_down, b_down)))
    sequences = tokens.astype(jnp.float32).reshape(SEQS, SEQ_LEN, D)
    time_steps = timestep.astype(jnp.float32)

    def whole(seq_inputs, weights):

        def per_sequence(operands):
            return one_sequence(operands[0], operands[1], operands[2], weights)
        return lax.map(jax.checkpoint(per_sequence), (seq_inputs, piece_starts, time_steps))
    outputs, pullback = jax.vjp(whole, sequences, params)
    d_seq, d_params = pullback(cotangent.astype(jnp.float32).reshape(SEQS, SEQ_LEN, D))
    d_mod_w, d_mod_b, d_gain_attn, d_qkv, d_out_proj, d_gain_mlp, d_up, d_up_bias, d_down, d_down_bias = d_params
    return (outputs.reshape(TOKENS, D).astype(jnp.bfloat16), d_seq.reshape(TOKENS, D), d_mod_w, d_mod_b, d_gain_attn, d_qkv, d_out_proj, d_gain_mlp, d_up, d_up_bias, d_down, d_down_bias)
```

```python
import functools
import math

import jax
import jax.numpy as jnp
from jax import lax
from jax.experimental import pallas as pl
from jax.experimental.pallas import tpu as pltpu
from jax.sharding import PartitionSpec as P

D = 768
HEAD = 64
HALF = HEAD // 2
COND = 128
PIECE = 256
KEYS = 256
LANES = 128
SCORE = HEAD ** (-0.5) * math.log2(math.e)
MASKED = -1e30

precise = lax.Precision.HIGHEST
epsilon = 1e-05
f32 = jnp.float32
bf16 = jnp.bfloat16


def row_swap(value):
    return lax.ppermute(value, "row", [(0, 1), (1, 0)])


def dp_swap(value, bit):
    return lax.ppermute(value, "dp", [(i, i ^ (1 << bit)) for i in range(lax.axis_size("dp"))])


def col_swap(value, bit):
    return lax.ppermute(value, "col", [(i, i ^ (1 << bit)) for i in range(lax.axis_size("col"))])


def col_from(value, hop):
    size = lax.axis_size("col")
    return lax.ppermute(value, "col", [(i, (i + hop) % size) for i in range(size)]) if hop else value


def col_to(value, hop):
    size = lax.axis_size("col")
    return lax.ppermute(value, "col", [(i, (i - hop) % size) for i in range(size)]) if hop else value


def bits(axis):
    return lax.axis_size(axis).bit_length() - 1


def core_bit():
    return lax.axis_index("dp") % 2


def in_order(bit, mine, theirs):
    first = bit == 0
    return jnp.where(first, mine, theirs), jnp.where(first, theirs, mine)


def half_at(value, index, axis):
    size = value.shape[axis] // 2
    return lax.dynamic_slice_in_dim(value, index * size, size, axis)


def gather_pieces(mine, join_axis):
    cols = lax.axis_size("col")
    own = jnp.stack([col_from(mine, k) for k in range(cols)])
    other = row_swap(own)
    joined = jnp.concatenate([own, other], join_axis)
    return joined, dp_swap(joined, 0)


def scatter_pieces(mine, theirs, join_axis):
    cols = lax.axis_size("col")
    total = (mine.astype(f32) + dp_swap(theirs, 0).astype(f32)).astype(bf16)
    own, other = jnp.split(total, 2, join_axis)
    total = (own.astype(f32) + row_swap(other).astype(f32)).astype(bf16)
    total = sum(col_to(total[k], k).astype(f32) for k in range(cols))
    for bit in range(1, bits("dp")):
        total = total + dp_swap(total, bit)
    return in_order(core_bit(), total, dp_swap(total, 0))


def place_stripes(scalars, own_refs, other_refs, keys, values_t, keys_t=None, values=None):
    row, col = scalars[0], scalars[1]
    count = len(own_refs)
    width = own_refs[0].shape[1]
    parts = width // LANES
    for hop in range(count):
        place = lax.rem(col + hop, count)
        for stripe, ref, offset in (
            (2 * place + row, own_refs[hop], HEAD),
            (2 * place + 1 - row, other_refs[hop], 0),
        ):
            start = pl.multiple_of(stripe * width, LANES)
            key_t = ref[offset : offset + HEAD, :]
            value_t = ref[offset + HEAD : offset + 2 * HEAD, :]
            keys[pl.ds(start, width), :] = key_t.astype(f32).T.astype(bf16)
            if values is not None:
                values[pl.ds(start, width), :] = value_t.astype(f32).T.astype(bf16)
            for part in range(parts):
                lanes = slice(part * LANES, (part + 1) * LANES)
                if values_t is not None:
                    values_t[stripe * parts + part] = value_t[:, lanes]
                if keys_t is not None:
                    keys_t[stripe * parts + part] = key_t[:, lanes]


def lane_block(ref, block):
    parts = KEYS // LANES
    return jnp.concatenate([ref[block * parts + part] for part in range(parts)], 1)


def forward_kernel(count, scalars, *refs):
    own_refs, other_refs = refs[:count], refs[count : 2 * count]
    limit_ref, out_ref, wide_ref, log_ref, keys, values_t = refs[2 * count :]
    width = own_refs[0].shape[1]
    place_stripes(scalars, own_refs, other_refs, keys, values_t)
    row, col = scalars[0], scalars[1]
    for hop in range(count):
        query_t = own_refs[hop][0:HEAD, :]
        limit = limit_ref[hop]
        first = (2 * lax.rem(col + hop, count) + row) * width

        def step(masked, block, carry):
            top, total, mixed = carry
            start = pl.multiple_of(block * KEYS, KEYS)
            scores = jnp.dot(keys[pl.ds(start, KEYS), :], query_t, preferred_element_type=f32) * SCORE
            if masked:
                place = start + lax.broadcasted_iota(jnp.int32, scores.shape, 0)
                scores = jnp.where(place <= limit, scores, MASKED)
            new_top = jnp.maximum(top, jnp.max(scores, 0, keepdims=True))
            fade = jnp.exp2(top - new_top)
            weight = jnp.exp2(scores - new_top)
            total = total * fade + jnp.sum(weight, 0, keepdims=True)
            mixed = mixed * fade + jnp.dot(
                lane_block(values_t, block), weight.astype(bf16), preferred_element_type=f32
            )
            return new_top, total, mixed

        carry = (
            jnp.full((1, width), MASKED, f32),
            jnp.zeros((1, width), f32),
            jnp.zeros((HEAD, width), f32),
        )
        whole = first // KEYS
        carry = lax.fori_loop(0, whole, functools.partial(step, False), carry)
        top, total, mixed = lax.fori_loop(whole, scalars[2 + hop], functools.partial(step, True), carry)
        mixed = mixed / total
        out_ref[hop] = mixed.astype(bf16)
        wide_ref[hop] = mixed
        log_ref[hop] = top + jnp.log2(total)


def backward_kernel(count, scalars, *refs):
    own_refs, other_refs, grad_refs = refs[:count], refs[count : 2 * count], refs[2 * count : 3 * count]
    (wide_ref, log_ref, limit_ref, turn_ref, d_query_ref, d_own_ref, d_other_ref) = refs[3 * count : 3 * count + 7]
    keys, values, keys_t, d_keys, d_values = refs[3 * count + 7 :]
    width = own_refs[0].shape[1]
    place_stripes(scalars, own_refs, other_refs, keys, None, keys_t, values)
    row, col = scalars[0], scalars[1]
    d_keys[...] = jnp.zeros_like(d_keys)
    d_values[...] = jnp.zeros_like(d_values)

    def turn_back(vectors, stripe):
        cosine, sine = turn_ref[stripe, 0:HALF, :], turn_ref[stripe, HALF:HEAD, :]
        upper, lower = vectors[0:HALF], vectors[HALF:HEAD]
        return jnp.concatenate([upper * cosine + lower * sine, lower * cosine - upper * sine], 0)

    for hop in range(count):
        query_t = own_refs[hop][0:HEAD, :]
        grad_t = grad_refs[hop][...]
        query = query_t.astype(f32).T.astype(bf16)
        grad = grad_t.astype(f32).T.astype(bf16)
        drift = jnp.sum(grad_t.astype(f32) * wide_ref[hop], 0, keepdims=True)
        log_sum = log_ref[hop]
        limit = limit_ref[hop]
        stripe = 2 * lax.rem(col + hop, count) + row
        first = stripe * width

        def step(masked, block, d_query):
            start = pl.multiple_of(block * KEYS, KEYS)
            rows = pl.ds(start, KEYS)
            scores = jnp.dot(keys[rows, :], query_t, preferred_element_type=f32) * SCORE
            weight = jnp.exp2(scores - log_sum)
            if masked:
                place = start + lax.broadcasted_iota(jnp.int32, scores.shape, 0)
                weight = jnp.where(place <= limit, weight, 0.0)
            d_weight = jnp.dot(values[rows, :], grad_t, preferred_element_type=f32)
            d_scores = (weight * (d_weight - drift)).astype(bf16)
            d_values[rows, :] += jnp.dot(weight.astype(bf16), grad, preferred_element_type=f32)
            d_keys[rows, :] += jnp.dot(d_scores, query, preferred_element_type=f32)
            return d_query + jnp.dot(lane_block(keys_t, block), d_scores, preferred_element_type=f32)

        d_query = jnp.zeros((HEAD, width), f32)
        whole = first // KEYS
        d_query = lax.fori_loop(0, whole, functools.partial(step, False), d_query)
        d_query = lax.fori_loop(whole, scalars[2 + hop], functools.partial(step, True), d_query)
        d_query_ref[hop] = turn_back(d_query * HEAD ** (-0.5), stripe).astype(bf16)

    for hop in range(count):
        place = lax.rem(col + hop, count)
        for stripe, ref in ((2 * place + row, d_own_ref), (2 * place + 1 - row, d_other_ref)):
            start = pl.multiple_of(stripe * width, LANES)
            d_key = d_keys[pl.ds(start, width), :].T * HEAD ** (-0.5)
            ref[hop, 0:HEAD, :] = turn_back(d_key, stripe).astype(ref.dtype)
            ref[hop, HEAD : 2 * HEAD, :] = d_values[pl.ds(start, width), :].T.astype(ref.dtype)


def vmem(count):
    return [pl.BlockSpec(memory_space=pltpu.VMEM)] * count


def attention_forward(scalars, own, other, limit):
    count = len(own)
    width = own[0].shape[1]
    seq_len = 2 * count * width
    return pl.pallas_call(
        functools.partial(forward_kernel, count),
        in_specs=[pl.BlockSpec(memory_space=pltpu.SMEM)] + vmem(2 * count + 1),
        out_specs=vmem(3),
        out_shape=[
            jax.ShapeDtypeStruct((count, HEAD, width), bf16),
            jax.ShapeDtypeStruct((count, HEAD, width), f32),
            jax.ShapeDtypeStruct((count, 1, width), f32),
        ],
        scratch_shapes=[
            pltpu.VMEM((seq_len, HEAD), bf16),
            pltpu.VMEM((seq_len // LANES, HEAD, LANES), bf16),
        ],
        cost_estimate=pl.CostEstimate(flops=8_000_000_000, bytes_accessed=3_000_000, transcendentals=3_000_000),
        name="attend",
    )(scalars, *own, *other, limit)


def attention_backward(scalars, own, other, grads, wide, log_sum, limit, turns):
    count = len(own)
    width = own[0].shape[1]
    seq_len = 2 * count * width
    return pl.pallas_call(
        functools.partial(backward_kernel, count),
        in_specs=[pl.BlockSpec(memory_space=pltpu.SMEM)] + vmem(3 * count + 4),
        out_specs=vmem(3),
        out_shape=[
            jax.ShapeDtypeStruct((count, HEAD, width), bf16),
            jax.ShapeDtypeStruct((count, 2 * HEAD, width), f32),
            jax.ShapeDtypeStruct((count, 2 * HEAD, width), bf16),
        ],
        scratch_shapes=[
            pltpu.VMEM((seq_len, HEAD), bf16),
            pltpu.VMEM((seq_len, HEAD), bf16),
            pltpu.VMEM((seq_len // LANES, HEAD, LANES), bf16),
            pltpu.VMEM((seq_len, HEAD), f32),
            pltpu.VMEM((seq_len, HEAD), f32),
        ],
        cost_estimate=pl.CostEstimate(flops=16_000_000_000, bytes_accessed=4_000_000, transcendentals=3_000_000),
        name="attend_back",
    )(scalars, *own, *other, *grads, wide, log_sum, limit, turns)


def contract(first, second, first_axis, second_axis):
    return lax.dot_general(
        first, second, (((first_axis,), (second_axis,)), ((), ())), preferred_element_type=f32
    )


def feed_kernel(h_ref, df_ref, up_ref, bias_ref, down_ref, f_ref, dh_ref, d_up_ref, d_down_ref, d_bias_ref):
    step = pl.program_id(0)

    @pl.when(step == 0)
    def _():
        f_ref[...] = jnp.zeros_like(f_ref)
        dh_ref[...] = jnp.zeros_like(dh_ref)

    h = h_ref[...]
    df = df_ref[...]
    up = up_ref[0]
    down = down_ref[0]
    hidden = contract(h, up, 1, 0) + bias_ref[0]
    squared = hidden * hidden
    bent = jnp.tanh(0.79788456 * hidden * (1.0 + 0.044715 * squared))
    active = (0.5 * hidden * (1.0 + bent)).astype(bf16)
    slope = 0.5 * (1.0 + bent) + 0.5 * hidden * (1.0 - bent * bent) * (
        0.79788456 * (1.0 + 3.0 * 0.044715 * squared)
    )
    f_ref[...] += contract(active, down, 1, 0)
    d_hidden_wide = slope * contract(df, down, 1, 1)
    d_hidden = d_hidden_wide.astype(bf16)
    d_bias_ref[0] = jnp.sum(d_hidden.astype(f32), 0, keepdims=True)
    dh_ref[...] += contract(d_hidden, up, 1, 1)
    d_down_ref[0] = contract(active, df, 0, 0).astype(bf16)
    d_up_ref[0] = contract(h, d_hidden, 0, 0).astype(bf16)


def feed_forward(h, df, up, bias, down):
    blocks, width, hidden = up.shape
    rows = h.shape[0]
    whole = pl.BlockSpec((rows, width), lambda b: (0, 0))
    return pl.pallas_call(
        feed_kernel,
        grid=(blocks,),
        in_specs=[
            whole,
            whole,
            pl.BlockSpec((1, width, hidden), lambda b: (b, 0, 0)),
            pl.BlockSpec((1, 1, hidden), lambda b: (b, 0, 0)),
            pl.BlockSpec((1, hidden, width), lambda b: (b, 0, 0)),
        ],
        out_specs=[
            whole,
            whole,
            pl.BlockSpec((1, width, hidden), lambda b: (b, 0, 0)),
            pl.BlockSpec((1, hidden, width), lambda b: (b, 0, 0)),
            pl.BlockSpec((1, 1, hidden), lambda b: (b, 0, 0)),
        ],
        out_shape=[
            jax.ShapeDtypeStruct((rows, width), f32),
            jax.ShapeDtypeStruct((rows, width), f32),
            jax.ShapeDtypeStruct(up.shape, bf16),
            jax.ShapeDtypeStruct(down.shape, bf16),
            jax.ShapeDtypeStruct((blocks, 1, hidden), f32),
        ],
        cost_estimate=pl.CostEstimate(
            flops=12 * rows * width * hidden * blocks, bytes_accessed=24_000_000, transcendentals=1_000_000
        ),
        name="feed",
    )(h, df, up, bias, down)


def embed_time(time_step):
    half_size = COND // 2
    frequency = jnp.exp(-math.log(10000.0) * jnp.arange(half_size, dtype=f32) / half_size)
    angles = time_step * frequency
    return jax.nn.silu(jnp.concatenate([jnp.cos(angles), jnp.sin(angles)]))


def norm_forward(values, gain, shift, scale):
    mean = jnp.mean(values, -1, keepdims=True)
    centered = values - mean
    inv_std = lax.rsqrt(jnp.mean(centered * centered, -1, keepdims=True) + epsilon)
    normed = centered * inv_std
    return normed, inv_std, (normed * gain * (1.0 + scale) + shift).astype(bf16)


def norm_backward(upstream, normed, inv_std, gain, scale):
    scaled = upstream * (gain * (1.0 + scale))
    mean_grad = jnp.mean(scaled, -1, keepdims=True)
    mean_proj = jnp.mean(scaled * normed, -1, keepdims=True)
    return (
        inv_std * (scaled - mean_grad - normed * mean_proj),
        jnp.sum(upstream, 0),
        jnp.sum(upstream * normed, 0),
    )


def rotate(first, second, cosine, sine):
    return first * cosine - second * sine, second * cosine + first * sine


def shards(
    tokens, cotangent, timestep, piece_starts, w_mod, b_mod, gain_attn, w_qkv, w_out, gain_mlp, w_up, b_up, w_down, b_down
):
    cols = lax.axis_size("col")
    row, col, core = lax.axis_index("row"), lax.axis_index("col"), core_bit()
    block_rows, part = tokens.shape
    width = block_rows // 2
    slots = w_qkv.shape[0] // (3 * HEAD)

    def half_rows(block):
        other = row_swap(half_at(block, 1 - row, 0))
        return jnp.concatenate([half_at(block, row, 0), other], 1).astype(f32)

    residual = half_rows(tokens)
    condition = embed_time(timestep[0].astype(f32))
    modulation = jnp.einsum("k,kjd->jd", condition, w_mod.astype(f32), precision=precise) + b_mod
    small = jnp.concatenate([modulation, gain_attn[None], gain_mlp[None], b_down[None]], 0)
    small = jnp.concatenate([small, row_swap(small)], 1)
    shift_attn, scale_attn, gate_attn, shift_mlp, scale_mlp, gate_mlp, gain_a, gain_m, bias_down = (
        small[i : i + 1] for i in range(9)
    )

    normed_one, inv_one, h_one = norm_forward(residual, gain_a, shift_attn, scale_attn)

    lane = jnp.arange(width, dtype=jnp.int32)
    frequency = jnp.exp(-math.log(10000.0) * jnp.arange(HALF, dtype=f32) / HALF)
    places = jnp.arange(2 * cols, dtype=jnp.int32)[:, None] * width + lane[None]
    angles = places.astype(f32)[:, None, :] * frequency[None, :, None]
    turns = jnp.concatenate([jnp.cos(angles), jnp.sin(angles)], 1)
    here = lax.dynamic_index_in_dim(turns, 2 * col + row, 0, keepdims=False)
    cosine, sine = here[:HALF], here[HALF:]
    own_stripes = 2 * ((col + jnp.arange(cols, dtype=jnp.int32)) % cols) + row
    own_places = own_stripes[:, None] * width + lane[None]
    starts = piece_starts[0]
    inside = (own_places[..., None] >= starts) & (own_places[..., None] < starts + PIECE)
    limit = jnp.max(jnp.where(inside, starts + PIECE - 1, own_places[..., None]), -1)
    scalars = jnp.concatenate([row[None], col[None], jnp.max(limit, 1) // KEYS + 1]).astype(jnp.int32)
    limit = limit[:, None, :]

    w_qkv_parts = w_qkv.reshape(slots, 3, 2, HALF, part)
    w_slots, own_heads, other_heads, forward = [], [], [], []
    for slot in range(slots):
        mine = lax.dynamic_index_in_dim(w_qkv_parts[slot], core, 1, keepdims=False).reshape(3 * HALF, part)
        mine, theirs = gather_pieces(mine, 2)
        lower, upper = in_order(
            core, mine.reshape(cols, 3, HALF, 2 * part), theirs.reshape(cols, 3, HALF, 2 * part)
        )
        weight = jnp.stack([lower, upper], 2).reshape(cols * 3 * HEAD, 2 * part)
        w_slots.append(weight)
        projected = contract(weight, h_one, 1, 1).reshape(cols, 3, 2, HALF, width)
        first, second = projected[:, :2, 0], projected[:, :2, 1]
        first, second = rotate(first, second, cosine, sine)
        turned = jnp.stack([first, second], 2)
        pieces = jnp.concatenate([turned, projected[:, 2:]], 1).reshape(cols, 3 * HEAD, width).astype(bf16)
        own = [col_to(pieces[k], k) for k in range(cols)]
        other = [row_swap(piece[HEAD:]) for piece in own]
        own_heads.append(own)
        other_heads.append(other)
        forward.append(attention_forward(scalars, own, other, limit))

    mixed = jnp.stack(
        [jnp.stack([col_from(forward[slot][0][k], k) for k in range(cols)]) for slot in range(slots)], 1
    ).reshape(cols * slots * HEAD, width)

    mine, theirs = gather_pieces(half_at(w_out, core, 0), 2)
    w_out_all = jnp.stack(in_order(core, mine, theirs), 1).reshape(cols * slots * HEAD, 2 * part)
    up = jnp.concatenate(gather_pieces(half_at(w_up, core, 1), 1), 0)
    down = jnp.concatenate(gather_pieces(half_at(w_down, core, 0), 2), 0)
    bias = jnp.stack([col_from(b_up[None], k) for k in range(cols)])
    bias = jnp.concatenate([half_at(bias, core, 2), half_at(bias, 1 - core, 2)], 0).astype(f32)

    attended = contract(mixed, w_out_all, 0, 0)
    middle = residual + gate_attn * attended
    normed_two, inv_two, h_two = norm_forward(middle, gain_m, shift_mlp, scale_mlp)
    upstream = half_rows(cotangent)
    d_branch = (upstream * gate_mlp).astype(bf16)
    branch, d_h_two, d_up, d_down, d_bias = feed_forward(h_two, d_branch, up, bias, down)
    branch = branch + bias_down
    block_out = (middle + gate_mlp * branch).astype(bf16)

    d_middle, sum_two, proj_two = norm_backward(d_h_two, normed_two, inv_two, gain_m, scale_mlp)
    d_middle = d_middle + upstream
    d_attended = (d_middle * gate_attn).astype(bf16)
    d_mixed = contract(w_out_all, d_attended, 1, 1).astype(bf16).reshape(cols, slots, HEAD, width)
    d_out = contract(mixed, d_attended, 1, 0).astype(bf16).reshape(cols, 2, slots * HEAD // 2, 2 * part)

    def halves(value, axis):
        return (
            lax.dynamic_index_in_dim(value, core, axis, keepdims=False),
            lax.dynamic_index_in_dim(value, 1 - core, axis, keepdims=False),
        )

    d_h_one = 0.0
    d_qkv = []
    for slot in range(slots):
        grads = [col_to(d_mixed[k, slot], k) for k in range(cols)]
        d_query, d_own, d_other = attention_backward(
            scalars, own_heads[slot], other_heads[slot], grads, forward[slot][1], forward[slot][2], limit, turns
        )
        d_keys = (d_own + row_swap(d_other).astype(f32)).astype(bf16)
        pieces = jnp.concatenate([d_query, d_keys], 1)
        back = jnp.stack([col_from(pieces[k], k) for k in range(cols)]).reshape(cols * 3 * HEAD, width)
        d_h_one = d_h_one + contract(back, w_slots[slot], 0, 0)
        grad = contract(back, h_one, 1, 0).astype(bf16).reshape(cols, 3, 2, HALF, 2 * part)
        mine, theirs = halves(grad, 2)
        lower, upper = scatter_pieces(
            mine.reshape(cols, 3 * HALF, 2 * part), theirs.reshape(cols, 3 * HALF, 2 * part), 2
        )
        d_qkv.append(
            jnp.stack([lower.reshape(3, HALF, part), upper.reshape(3, HALF, part)], 1).reshape(3 * HEAD, part)
        )
    d_qkv = jnp.concatenate(d_qkv, 0)

    d_input, sum_one, proj_one = norm_backward(d_h_one, normed_one, inv_one, gain_a, scale_attn)
    d_tokens = d_input + d_middle

    d_up = jnp.concatenate(scatter_pieces(d_up[:cols], d_up[cols:], 1), 1)
    d_down = jnp.concatenate(scatter_pieces(d_down[:cols], d_down[cols:], 2), 0)
    d_out_proj = jnp.concatenate(scatter_pieces(*halves(d_out, 1), 2), 0)

    def whole_rows(value):
        own, other = value[:, :part], row_swap(value[:, part:])
        return jnp.concatenate(in_order(row, own, other), 0)

    sums = jnp.stack(
        [
            sum_one,
            proj_one,
            jnp.sum(d_middle * attended, 0),
            sum_two,
            proj_two,
            jnp.sum(upstream * branch, 0),
            jnp.sum(d_branch.astype(f32), 0),
        ]
    )
    sums = sums[:, :part] + row_swap(sums[:, part:])
    for bit in range(bits("col")):
        sums = sums + col_swap(sums, bit)
    per_seq = jnp.stack(
        [
            sums[0],
            sums[1] * gain_attn,
            sums[2],
            sums[3],
            sums[4] * gain_mlp,
            sums[5],
            sums[1] * (1.0 + modulation[1]),
            sums[4] * (1.0 + modulation[4]),
            sums[6],
        ]
    )[None]
    conditions = condition[None]
    index = lax.axis_index("dp")
    for bit in range(bits("dp")):
        place = (index >> bit) % 2
        per_seq = jnp.concatenate(in_order(place, per_seq, dp_swap(per_seq, bit)), 0)
        conditions = jnp.concatenate(in_order(place, conditions, dp_swap(conditions, bit)), 0)
    d_mod_w = sum(conditions[s][:, None, None] * per_seq[s, :6][None] for s in range(per_seq.shape[0]))
    totals = jnp.sum(per_seq, 0)

    d_bias = d_bias.reshape(2, cols, d_bias.shape[-1])
    d_bias = jnp.stack(in_order(core, d_bias[0], d_bias[1]), 1)
    d_bias = d_bias + row_swap(d_bias)
    d_bias = sum(col_to(d_bias[k], k) for k in range(cols))
    for bit in range(bits("dp")):
        d_bias = d_bias + dp_swap(d_bias, bit)

    return (
        whole_rows(block_out),
        whole_rows(d_tokens),
        d_mod_w,
        totals[:6],
        totals[6],
        d_qkv,
        d_out_proj,
        totals[7],
        d_up,
        d_bias.reshape(-1),
        d_down,
        totals[8],
    )


def solution(mesh):
    blocks = P(("dp", "col"), "row")
    return jax.shard_map(
        shards,
        mesh=mesh,
        in_specs=(
            blocks,
            blocks,
            P("dp"),
            P("dp", None),
            P(None, None, "row"),
            P(None, "row"),
            P("row"),
            P("col", "row"),
            P("col", "row"),
            P("row"),
            P("row", "col"),
            P("col"),
            P("col", "row"),
            P("row"),
        ),
        out_specs=(
            blocks,
            blocks,
            P(None, None, "row"),
            P(None, "row"),
            P("row"),
            P("col", "row"),
            P("col", "row"),
            P("row"),
            P("row", "col"),
            P("col"),
            P("col", "row"),
            P("row"),
        ),
        check_vma=False,
    )
```

```python
import functools
import math

import jax
import jax.numpy as jnp
from jax import lax
from jax.experimental import pallas as pl
from jax.experimental.pallas import tpu as pltpu
from jax.sharding import PartitionSpec as P

D = 768
HEAD = 64
HALF = HEAD // 2
COND = 128
PIECE = 256
KEYS = 256
LANES = 128
PAD = 16
CHUNK = 128
SLICES = 4
SCORE = HEAD ** (-0.5) * math.log2(math.e)
MASKED = -1e30

precise = lax.Precision.HIGHEST
epsilon = 1e-05
f32 = jnp.float32
bf16 = jnp.bfloat16


def row_swap(value):
    return lax.ppermute(value, "row", [(0, 1), (1, 0)])


def dp_swap(value, bit):
    return lax.ppermute(value, "dp", [(i, i ^ (1 << bit)) for i in range(lax.axis_size("dp"))])


def col_swap(value, bit):
    return lax.ppermute(value, "col", [(i, i ^ (1 << bit)) for i in range(lax.axis_size("col"))])


def col_from(value, hop):
    size = lax.axis_size("col")
    return lax.ppermute(value, "col", [(i, (i + hop) % size) for i in range(size)]) if hop else value


def col_trade(value):
    return lax.all_to_all(value, "col", 0, 0, tiled=True)


def bits(axis):
    return lax.axis_size(axis).bit_length() - 1


def dp_bit(bit):
    return (lax.axis_index("dp") >> bit) % 2


def in_order(bit, mine, theirs):
    first = bit == 0
    return jnp.where(first, mine, theirs), jnp.where(first, theirs, mine)


def half_at(value, index, axis):
    size = value.shape[axis] // 2
    return lax.dynamic_slice_in_dim(value, index * size, size, axis)


def gather_halves(mine, order):
    pieces = [col_from(mine, k) for k in range(lax.axis_size("col"))]
    yield
    own = jnp.stack(order.next(pieces))
    order.done(own)
    other = row_swap(own)
    own_far = dp_swap(own, 0)
    yield
    other = order.next(other)
    order.done(other)
    yield [own, other, own_far, dp_swap(other, 0)]


def scatter_halves(mine, theirs, order):
    def added(first, second):
        return (first.astype(f32) + second.astype(f32)).astype(bf16)

    heard = dp_swap(theirs, 0)
    yield
    heard = order.next(heard)
    keep, other = added(mine[0], heard[0]), added(mine[1], heard[1])
    order.done(keep, other)
    heard = row_swap(other)
    yield
    total = added(keep, order.next(heard))
    order.done(total)
    parts = col_trade(total)
    yield
    total = jnp.sum(order.next(parts).astype(f32), 0)
    order.done(total)
    for bit in range(1, bits("dp")):
        total = total + dp_swap(total, bit)
    yield
    yield in_order(dp_bit(0), total, dp_swap(total, 0))


def after(value, *others):
    return lax.optimization_barrier((value, others))[0]


class Order:
    def __init__(self):
        self.last = ()

    def next(self, value):
        return after(value, self.last)

    def done(self, *results):
        self.last = results


def contract(first, second, first_axis, second_axis):
    return lax.dot_general(
        first, second, (((first_axis,), (second_axis,)), ((), ())), preferred_element_type=f32
    )


def turned(vectors):
    return vectors.astype(f32).T.astype(bf16)


def in_vmem(count):
    return [pl.BlockSpec(memory_space=pltpu.VMEM)] * count


def in_place(count):
    return [pl.BlockSpec(memory_space=pl.ANY)] * count


SCALARS = pl.BlockSpec(memory_space=pltpu.SMEM)


def like(shape, dtype):
    return jax.ShapeDtypeStruct(shape, dtype)


def cost(flops, moved, powers=0):
    return pl.CostEstimate(flops=flops, bytes_accessed=moved, transcendentals=powers)


def project_kernel(count, slots, scalars, h_ref, turn_ref, *refs):
    sources, w_ref, out_ref, sems = refs[:4], refs[4], refs[5], refs[6]
    part = sources[0].shape[2]
    rows = 3 * HALF
    copies = []
    for index, source in enumerate(sources):
        o, core = index % 2, index // 2
        place = scalars[2] ^ core
        for k in range(count):
            column = lax.rem(scalars[1] + count - k, count)
            for s in range(slots):
                start = pl.multiple_of(column * 3 * HEAD + place * rows, PAD)
                copies.append(
                    pltpu.make_async_copy(
                        source.at[k, pl.ds(s * rows, rows), :],
                        w_ref.at[s, pl.ds(start, rows), pl.ds(o * part, part)],
                        sems.at[len(copies)],
                    )
                )
    for copy in copies:
        copy.start()
    for copy in copies:
        copy.wait()
    h = h_ref[...]
    cosine, sine = turn_ref[0:HALF, :], turn_ref[HALF:HEAD, :]
    for s in range(slots):
        base = s * 3 * HEAD
        for k in range(count):
            values = contract(w_ref[s, k * 3 * HEAD : (k + 1) * 3 * HEAD, :], h, 1, 1)
            for i in range(2):
                low, middle, high = i * HEAD, i * HEAD + HALF, (i + 1) * HEAD
                first, second = values[low:middle], values[middle:high]
                out_ref[k, base + low : base + middle, :] = (first * cosine - second * sine).astype(bf16)
                out_ref[k, base + middle : base + high, :] = (second * cosine + first * sine).astype(bf16)
            out_ref[k, base + 2 * HEAD : base + 3 * HEAD, :] = values[2 * HEAD :].astype(bf16)


def project(scalars, h, turn, sources, slots):
    count, _, part = sources[0].shape
    width = h.shape[0]
    return pl.pallas_call(
        functools.partial(project_kernel, count, slots),
        in_specs=[SCALARS] + in_vmem(2) + in_place(len(sources)),
        out_specs=in_vmem(2),
        out_shape=[
            like((slots, count * 3 * HEAD, 2 * part), bf16),
            like((count, slots * 3 * HEAD, width), bf16),
        ],
        scratch_shapes=[pltpu.SemaphoreType.DMA((len(sources) * count * slots,))],
        cost_estimate=cost(slots * 2 * count * 3 * HEAD * 2 * part * width, 3_000_000 * slots),
        name="project",
    )(scalars, h, turn, *sources)


def pack_kernel(offset, _, own_ref, out_ref):
    for index in range(own_ref.shape[0]):
        out_ref[index] = own_ref[index, offset + HEAD : offset + 3 * HEAD, :]


def pack(scalars, own, offset):
    count, _, width = own.shape
    return pl.pallas_call(
        functools.partial(pack_kernel, offset),
        in_specs=[SCALARS] + in_vmem(1),
        out_specs=in_vmem(1)[0],
        out_shape=like((count, 2 * HEAD, width), bf16),
        cost_estimate=cost(1000, 1_000_000),
        name="pack",
    )(scalars, own)


def merge_kernel(_, d_query_ref, d_own_ref, heard_ref, out_ref):
    for index in range(out_ref.shape[0]):
        out_ref[index, :HEAD, :] = d_query_ref[index]
        out_ref[index, HEAD:, :] = (d_own_ref[index] + heard_ref[index].astype(f32)).astype(bf16)


def merge(scalars, d_query, d_own, heard):
    count, _, width = d_query.shape
    return pl.pallas_call(
        merge_kernel,
        in_specs=[SCALARS] + in_vmem(3),
        out_specs=in_vmem(1)[0],
        out_shape=like((count, 3 * HEAD, width), bf16),
        cost_estimate=cost(1000, 2_000_000),
        name="merge",
    )(scalars, d_query, d_own, heard)


def place_stripes(scalars, own_ref, offset, other_ref, keys, values_t, keys_t=None, values=None):
    row = scalars[0]
    count, _, width = own_ref.shape
    parts = width // LANES
    for place in range(count):
        for stripe, ref, base in (
            (2 * place + row, own_ref.at[place], offset + HEAD),
            (2 * place + 1 - row, other_ref.at[place], 0),
        ):
            start = pl.multiple_of(stripe * width, LANES)
            key_t = ref[base : base + HEAD, :]
            value_t = ref[base + HEAD : base + 2 * HEAD, :]
            keys[pl.ds(start, width), :] = turned(key_t)
            if values is not None:
                values[pl.ds(start, width), :] = turned(value_t)
            for part in range(parts):
                lanes = slice(part * LANES, (part + 1) * LANES)
                if values_t is not None:
                    values_t[stripe * parts + part] = value_t[:, lanes]
                if keys_t is not None:
                    keys_t[stripe * parts + part] = key_t[:, lanes]


def lane_block(ref, block):
    parts = KEYS // LANES
    return jnp.concatenate([ref[block * parts + part] for part in range(parts)], 1)


def attend_kernel(offset, earlier, scalars, own_ref, other_ref, limit_ref, *refs):
    before_ref, (out_ref, wide_ref, log_ref, keys, values_t) = refs[:earlier], refs[earlier:]
    count, _, width = own_ref.shape
    place_stripes(scalars, own_ref, offset, other_ref, keys, values_t)
    row = scalars[0]

    def stripe(place, _):
        query_t = own_ref[place, offset : offset + HEAD, :]
        limit = limit_ref[place]
        first = (2 * place + row) * width

        def step(masked, block, carry):
            top, total, mixed = carry
            start = pl.multiple_of(block * KEYS, KEYS)
            scores = jnp.dot(keys[pl.ds(start, KEYS), :], query_t, preferred_element_type=f32) * SCORE
            if masked:
                key = start + lax.broadcasted_iota(jnp.int32, scores.shape, 0)
                scores = jnp.where(key <= limit, scores, MASKED)
            new_top = jnp.maximum(top, jnp.max(scores, 0, keepdims=True))
            fade = jnp.exp2(top - new_top)
            weight = jnp.exp2(scores - new_top)
            total = total * fade + jnp.sum(weight, 0, keepdims=True)
            mixed = mixed * fade + jnp.dot(
                lane_block(values_t, block), weight.astype(bf16), preferred_element_type=f32
            )
            return new_top, total, mixed

        carry = (
            jnp.full((1, width), MASKED, f32),
            jnp.zeros((1, width), f32),
            jnp.zeros((HEAD, width), f32),
        )
        whole = first // KEYS
        carry = lax.fori_loop(0, whole, functools.partial(step, False), carry)
        top, total, mixed = lax.fori_loop(whole, scalars[3 + place], functools.partial(step, True), carry)
        mixed = mixed / total
        wide_ref[place] = mixed
        log_ref[place] = top + jnp.log2(total)
        return 0

    lax.fori_loop(0, count, stripe, 0)
    rows = out_ref.shape[1]
    for place in range(count):
        out_ref[place, rows - HEAD :, :] = wide_ref[place].astype(bf16)
        if earlier:
            out_ref[place, : rows - HEAD, :] = before_ref[0][place]


def attend(scalars, own, offset, other, limit, earlier):
    count, _, width = own.shape
    seq_len = 2 * count * width
    rows = HEAD + (earlier[0].shape[1] if earlier else 0)
    return pl.pallas_call(
        functools.partial(attend_kernel, offset, len(earlier)),
        in_specs=[SCALARS] + in_vmem(3 + len(earlier)),
        out_specs=in_vmem(3),
        out_shape=[
            like((count, rows, width), bf16),
            like((count, HEAD, width), f32),
            like((count, 1, width), f32),
        ],
        scratch_shapes=[
            pltpu.VMEM((seq_len, HEAD), bf16),
            pltpu.VMEM((seq_len // LANES, HEAD, LANES), bf16),
        ],
        cost_estimate=cost(8_000_000_000, 3_000_000, 3_000_000),
        name="attend",
    )(scalars, own, other, limit, *earlier)


def attend_back_kernel(
    offset,
    grad_offset,
    scalars,
    own_ref,
    other_ref,
    grad_ref,
    wide_ref,
    log_ref,
    limit_ref,
    turn_ref,
    d_query_ref,
    d_own_ref,
    d_other_ref,
    keys,
    values,
    keys_t,
    d_keys,
    d_values,
):
    count, _, width = own_ref.shape
    place_stripes(scalars, own_ref, offset, other_ref, keys, None, keys_t, values)
    row = scalars[0]
    d_keys[...] = jnp.zeros_like(d_keys)
    d_values[...] = jnp.zeros_like(d_values)

    def turn_back(vectors, stripe):
        cosine, sine = turn_ref[stripe, 0:HALF, :], turn_ref[stripe, HALF:HEAD, :]
        upper, lower = vectors[0:HALF], vectors[HALF:HEAD]
        return jnp.concatenate([upper * cosine + lower * sine, lower * cosine - upper * sine], 0)

    def of_stripe(place, _):
        query_t = own_ref[place, offset : offset + HEAD, :]
        grad_t = grad_ref[place, grad_offset : grad_offset + HEAD, :]
        query = turned(query_t)
        grad = turned(grad_t)
        drift = jnp.sum(grad_t.astype(f32) * wide_ref[place], 0, keepdims=True)
        log_sum = log_ref[place]
        limit = limit_ref[place]
        stripe = 2 * place + row

        def step(masked, block, d_query):
            start = pl.multiple_of(block * KEYS, KEYS)
            rows = pl.ds(start, KEYS)
            scores = jnp.dot(keys[rows, :], query_t, preferred_element_type=f32) * SCORE
            weight = jnp.exp2(scores - log_sum)
            if masked:
                key = start + lax.broadcasted_iota(jnp.int32, scores.shape, 0)
                weight = jnp.where(key <= limit, weight, 0.0)
            d_weight = jnp.dot(values[rows, :], grad_t, preferred_element_type=f32)
            d_scores = (weight * (d_weight - drift)).astype(bf16)
            d_values[rows, :] += jnp.dot(weight.astype(bf16), grad, preferred_element_type=f32)
            d_keys[rows, :] += jnp.dot(d_scores, query, preferred_element_type=f32)
            return d_query + jnp.dot(lane_block(keys_t, block), d_scores, preferred_element_type=f32)

        d_query = jnp.zeros((HEAD, width), f32)
        whole = stripe * width // KEYS
        d_query = lax.fori_loop(0, whole, functools.partial(step, False), d_query)
        d_query = lax.fori_loop(whole, scalars[3 + place], functools.partial(step, True), d_query)
        d_query_ref[place] = turn_back(d_query * HEAD ** (-0.5), stripe).astype(bf16)
        return 0

    lax.fori_loop(0, count, of_stripe, 0)

    def finish(place, _):
        for stripe, ref in ((2 * place + row, d_own_ref), (2 * place + 1 - row, d_other_ref)):
            start = pl.multiple_of(stripe * width, LANES)
            d_key = d_keys[pl.ds(start, width), :].T * HEAD ** (-0.5)
            ref[place, 0:HEAD, :] = turn_back(d_key, stripe).astype(ref.dtype)
            ref[place, HEAD : 2 * HEAD, :] = d_values[pl.ds(start, width), :].T.astype(ref.dtype)
        return 0

    lax.fori_loop(0, count, finish, 0)


def attend_back(scalars, own, offset, other, grad, grad_offset, wide, log_sum, limit, turns):
    count, _, width = own.shape
    seq_len = 2 * count * width
    return pl.pallas_call(
        functools.partial(attend_back_kernel, offset, grad_offset),
        in_specs=[SCALARS] + in_vmem(7),
        out_specs=in_vmem(3),
        out_shape=[
            like((count, HEAD, width), bf16),
            like((count, 2 * HEAD, width), f32),
            like((count, 2 * HEAD, width), bf16),
        ],
        scratch_shapes=[
            pltpu.VMEM((seq_len, HEAD), bf16),
            pltpu.VMEM((seq_len, HEAD), bf16),
            pltpu.VMEM((seq_len // LANES, HEAD, LANES), bf16),
            pltpu.VMEM((seq_len, HEAD), f32),
            pltpu.VMEM((seq_len, HEAD), f32),
        ],
        cost_estimate=cost(16_000_000_000, 4_000_000, 3_000_000),
        name="attend_back",
    )(scalars, own, other, grad, wide, log_sum, limit, turns)


SMALL = 9
SHIFT_A, SCALE_A, GATE_A, SHIFT_M, SCALE_M, GATE_M, GAIN_A, GAIN_M, BIAS_DOWN = range(SMALL)


def middle_kernel(slots, scalars, x_own, x_other, g_own, g_other, small_ref, first_ref, last_ref, source, *refs):
    block_own, block_other, d_middle_ref, h_ref, df_ref, d_att_ref, active_ref, d_hidden_ref, mixed_ref, sums_ref = refs[:10]
    d_first, d_last, w_out, up, down, bias, attended_ref, mid_ref, f_ref, dh_ref, sems = refs[10:]
    width, part = x_own.shape
    count = first_ref.shape[0]
    out_rows = slots * HEAD // SLICES
    step_rows = part // 2
    copies = {"out": [], "up": [], "down": [], "bias": []}
    used = 0

    def copy(kind, origin, target):
        nonlocal used
        copies[kind].append(pltpu.make_async_copy(origin, target, sems.at[used]))
        used += 1

    for index in range(SLICES):
        y, core = index // 2, index % 2
        for o in range(2):
            lanes = pl.ds(o * part, part)
            for k in range(count):
                b = core * count + k
                origin = source.at[index, scalars[0] ^ o, k]
                start = k * slots * HEAD + (2 * core + y) * out_rows
                copy("out", origin.at[pl.ds(0, out_rows), :], w_out.at[pl.ds(start, out_rows), lanes])
                start = y * step_rows
                copy("down", origin.at[pl.ds(out_rows, step_rows), :], down.at[b, pl.ds(start, step_rows), lanes])
                copy(
                    "up",
                    origin.at[pl.ds(out_rows + step_rows, step_rows), :],
                    up.at[b, pl.ds(o * part + start, step_rows), :],
                )
                if o == 0 and y == 0:
                    copy("bias", origin.at[pl.ds(out_rows + 2 * step_rows, PAD), :], bias.at[b])
    for kind in copies:
        for each in copies[kind]:
            each.start()
    for k in range(count):
        base = k * slots * HEAD
        mixed_ref[base : base + (slots - 1) * HEAD, :] = first_ref[k]
        mixed_ref[base + (slots - 1) * HEAD : base + slots * HEAD, :] = last_ref[k]

    def small(index):
        return small_ref[index : index + 1, :]

    def wide_rows(own, other, rows):
        return jnp.concatenate([own[rows, :].astype(f32), other[rows, :].astype(f32)], 1)

    def norm(values, rows):
        mean = jnp.mean(values, 1, keepdims=True)
        centered = values - mean
        inv_std = lax.rsqrt(jnp.mean(centered * centered, 1, keepdims=True) + epsilon)
        return centered * inv_std, inv_std

    for each in copies["out"]:
        each.wait()
    attended_ref[...] = contract(mixed_ref[...], w_out[...], 0, 0)
    f_ref[...] = jnp.zeros_like(f_ref)
    dh_ref[...] = jnp.zeros_like(dh_ref)
    sums_ref[...] = jnp.zeros_like(sums_ref)

    def before(index, _):
        rows = pl.ds(pl.multiple_of(index * CHUNK, CHUNK), CHUNK)
        middle = wide_rows(x_own, x_other, rows) + small(GATE_A) * attended_ref[rows, :]
        mid_ref[rows, :] = middle
        normed, _ = norm(middle, rows)
        h_ref[rows, :] = (normed * (small(GAIN_M) * (1.0 + small(SCALE_M))) + small(SHIFT_M)).astype(bf16)
        df_ref[rows, :] = (wide_rows(g_own, g_other, rows) * small(GATE_M)).astype(bf16)
        return 0

    lax.fori_loop(0, width // CHUNK, before, 0)
    for kind in ("up", "down", "bias"):
        for each in copies[kind]:
            each.wait()

    def feed(b, _):
        h, df = h_ref[...], df_ref[...]
        u = contract(h, up[b], 1, 0) + bias[b][0:1, :].astype(f32)
        squared = u * u
        bent = jnp.tanh(0.79788456 * u * (1.0 + 0.044715 * squared))
        active = (0.5 * u * (1.0 + bent)).astype(bf16)
        slope = 0.5 * (1.0 + bent) + 0.5 * u * (1.0 - bent * bent) * (
            0.79788456 * (1.0 + 3.0 * 0.044715 * squared)
        )
        active_ref[b] = active
        d_hidden = (slope * contract(df, down[b], 1, 1)).astype(bf16)
        d_hidden_ref[b] = d_hidden
        f_ref[...] += contract(active, down[b], 1, 0)
        dh_ref[...] += contract(d_hidden, up[b], 1, 1)
        return 0

    lax.fori_loop(0, 2 * count, feed, 0)

    def after(index, _):
        rows = pl.ds(pl.multiple_of(index * CHUNK, CHUNK), CHUNK)
        middle = mid_ref[rows, :]
        branch = f_ref[rows, :] + small(BIAS_DOWN)
        out = (middle + small(GATE_M) * branch).astype(bf16)
        block_own[rows, :] = out[:, :part]
        block_other[rows, :] = out[:, part:]
        upstream = wide_rows(g_own, g_other, rows)
        normed, inv_std = norm(middle, rows)
        dh = dh_ref[rows, :]
        scaled = dh * (small(GAIN_M) * (1.0 + small(SCALE_M)))
        mean_grad = jnp.mean(scaled, 1, keepdims=True)
        mean_proj = jnp.mean(scaled * normed, 1, keepdims=True)
        d_middle = upstream + inv_std * (scaled - mean_grad - normed * mean_proj)
        d_middle_ref[rows, :] = d_middle
        d_att_ref[rows, :] = (d_middle * small(GATE_A)).astype(bf16)
        for i, value in enumerate(
            (d_middle * attended_ref[rows, :], dh, dh * normed, upstream * branch, df_ref[rows, :].astype(f32))
        ):
            sums_ref[i : i + 1, :] += jnp.sum(value, 0, keepdims=True)
        return 0

    lax.fori_loop(0, width // CHUNK, after, 0)
    d_att = d_att_ref[...]
    for k in range(count):
        base = k * slots * HEAD
        values = contract(w_out[base : base + slots * HEAD, :], d_att, 1, 1).astype(bf16)
        d_first[k] = values[: (slots - 1) * HEAD]
        d_last[k] = values[(slots - 1) * HEAD :]


def middle(scalars, x, g, small, first, last, source, slots):
    count = first.shape[0]
    width, part = x[0].shape
    blocks = 2 * count
    heads = count * slots * HEAD
    return pl.pallas_call(
        functools.partial(middle_kernel, slots),
        in_specs=[SCALARS] + in_vmem(7) + in_place(1),
        out_specs=in_vmem(12),
        out_shape=[
            like((width, part), bf16),
            like((width, part), bf16),
            like((width, 2 * part), f32),
            like((width, 2 * part), bf16),
            like((width, 2 * part), bf16),
            like((width, 2 * part), bf16),
            like((blocks, width, part), bf16),
            like((blocks, width, part), bf16),
            like((heads, width), bf16),
            like((8, 2 * part), f32),
            like((count, (slots - 1) * HEAD, width), bf16),
            like((count, HEAD, width), bf16),
        ],
        scratch_shapes=[
            pltpu.VMEM((heads, 2 * part), bf16),
            pltpu.VMEM((blocks, 2 * part, part), bf16),
            pltpu.VMEM((blocks, part, 2 * part), bf16),
            pltpu.VMEM((blocks, PAD, part), bf16),
            pltpu.VMEM((width, 2 * part), f32),
            pltpu.VMEM((width, 2 * part), f32),
            pltpu.VMEM((width, 2 * part), f32),
            pltpu.VMEM((width, 2 * part), f32),
            pltpu.SemaphoreType.DMA(((6 * SLICES + 2) * count,)),
        ],
        cost_estimate=cost(2 * width * (4 * blocks * part * 2 * part + 2 * heads * 2 * part), 14_000_000, 2_000_000),
        name="middle",
    )(scalars, *x, *g, small, first, last, source)


def grads_kernel(slots, scalars, h_ref, df_ref, d_att_ref, active_ref, d_hidden_ref, mixed_ref, out_ref, d_out):
    part = h_ref.shape[1] // 2
    count = active_ref.shape[0] // 2
    out_rows = slots * HEAD // SLICES
    step_rows = part // 2
    d_out[...] = contract(mixed_ref[...], d_att_ref[...], 1, 0).astype(bf16)

    def of_block(b, _):
        core, k = b // count, b % count
        d_hidden = d_hidden_ref[b]
        d_up = contract(h_ref[...], d_hidden, 0, 0).astype(bf16)
        d_down = contract(active_ref[b], df_ref[...], 0, 0).astype(bf16)
        d_bias = jnp.broadcast_to(jnp.sum(d_hidden.astype(f32), 0, keepdims=True), (PAD, part)).astype(bf16)
        for y in range(2):
            start = pl.multiple_of(k * slots * HEAD + (2 * core + y) * out_rows, PAD)
            out_part = d_out[pl.ds(start, out_rows), :]
            for o in range(2):
                target = out_ref.at[2 * y + core, scalars[0] ^ o, k]
                lanes = slice(o * part, (o + 1) * part)
                start = o * part + y * step_rows
                target[:out_rows, :] = out_part[:, lanes]
                target[out_rows : out_rows + step_rows, :] = d_down[y * step_rows : (y + 1) * step_rows, lanes]
                target[out_rows + step_rows : out_rows + 2 * step_rows, :] = d_up[start : start + step_rows]
                target[out_rows + 2 * step_rows :, :] = d_bias
        return 0

    lax.fori_loop(0, 2 * count, of_block, 0)


def weight_grads(scalars, h, df, d_att, active, d_hidden, mixed, slots):
    count = active.shape[0] // 2
    width, whole = h.shape
    part = whole // 2
    return pl.pallas_call(
        functools.partial(grads_kernel, slots),
        in_specs=[SCALARS] + in_vmem(6),
        out_specs=in_vmem(1)[0],
        out_shape=like((SLICES, 2, count, slots * HEAD // SLICES + part + PAD, part), bf16),
        scratch_shapes=[pltpu.VMEM((mixed.shape[0], whole), bf16)],
        cost_estimate=cost(2 * width * (4 * count * part * whole + mixed.shape[0] * whole), 20_000_000),
        name="weight_grads",
    )(scalars, h, df, d_att, active, d_hidden, mixed)


def unproject_kernel(scalars, h_ref, w_ref, *refs):
    slots = w_ref.shape[0]
    pieces, (dh_ref, mine, theirs, grad) = refs[:slots], refs[slots:]
    count, rows, width = pieces[0].shape
    part = h_ref.shape[1] // 2
    half = rows // 2
    dh = jnp.zeros(dh_ref.shape, f32)
    for s in range(slots):
        back = pieces[s][...].reshape(count * rows, width)
        dh = dh + contract(back, w_ref[s], 0, 0)
        grad[...] = contract(back, h_ref[...], 1, 0).astype(bf16)
        for core, target in enumerate((mine, theirs)):
            place = scalars[2] ^ core
            for k in range(count):
                start = pl.multiple_of(k * rows + place * half, PAD)
                values = grad[pl.ds(start, half), :]
                for o in range(2):
                    target[o, k, s * half : (s + 1) * half, :] = values[:, o * part : (o + 1) * part]
    dh_ref[...] = dh


def unproject(scalars, h, weight, pieces):
    width, whole = h.shape
    slots = len(pieces)
    count = pieces[0].shape[0]
    shape = like((2, count, slots * 3 * HALF, whole // 2), bf16)
    return pl.pallas_call(
        unproject_kernel,
        in_specs=[SCALARS] + in_vmem(2 + slots),
        out_specs=in_vmem(3),
        out_shape=[like((width, whole), f32), shape, shape],
        scratch_shapes=[pltpu.VMEM((weight.shape[1], whole), bf16)],
        cost_estimate=cost(slots * 4 * width * whole * weight.shape[1], 5_000_000 * slots),
        name="unproject",
    )(scalars, h, weight, *pieces)


def embed_time(time_step):
    half_size = COND // 2
    frequency = jnp.exp(-math.log(10000.0) * jnp.arange(half_size, dtype=f32) / half_size)
    angles = time_step * frequency
    return jax.nn.silu(jnp.concatenate([jnp.cos(angles), jnp.sin(angles)]))


def shards(
    tokens, cotangent, timestep, piece_starts, w_mod, b_mod, gain_attn, w_qkv, w_out, gain_mlp, w_up, b_up, w_down, b_down
):
    cols = lax.axis_size("col")
    row, col, core, far = lax.axis_index("row"), lax.axis_index("col"), dp_bit(0), dp_bit(1)
    block_rows, part = tokens.shape
    width = block_rows // 2
    slots = w_qkv.shape[0] // (3 * HEAD)

    def half_rows(block):
        return half_at(block, row, 0), row_swap(half_at(block, 1 - row, 0))

    x = half_rows(tokens)

    order = Order()

    w_parts = w_qkv.reshape(slots, 3 * HEAD, part)
    groups = [(0, 1), (1, slots)]
    blocks = [half_at(w_parts[low:high], core, 1).reshape(-1, part) for low, high in groups]

    def quarter_at(block):
        return half_at(half_at(block, core, 0), far, 0)

    bias = jnp.broadcast_to(half_at(b_up[None], core, 1), (PAD, part))
    rest = jnp.concatenate(
        [quarter_at(w_out), quarter_at(w_down), half_at(half_at(w_up, core, 1), far, 0), bias], 0
    )

    condition = embed_time(timestep[0].astype(f32))
    modulation = jnp.einsum("k,kjd->jd", condition, w_mod.astype(f32), precision=precise) + b_mod
    small = jnp.concatenate([modulation, gain_attn[None], gain_mlp[None], b_down[None]], 0)
    small = jnp.concatenate([small, row_swap(small)], 1)

    residual = jnp.concatenate(x, 1).astype(f32)
    centered = residual - jnp.mean(residual, -1, keepdims=True)
    inv_std = lax.rsqrt(jnp.mean(centered * centered, -1, keepdims=True) + epsilon)
    gain_one = small[GAIN_A] * (1.0 + small[SCALE_A])
    h_one = (centered * inv_std * gain_one + small[SHIFT_A]).astype(bf16)

    lane = jnp.arange(width, dtype=jnp.int32)
    frequency = jnp.exp(-math.log(10000.0) * jnp.arange(HALF, dtype=f32) / HALF)
    places = jnp.arange(2 * cols, dtype=jnp.int32)[:, None] * width + lane[None]
    angles = places.astype(f32)[:, None, :] * frequency[None, :, None]
    turns = jnp.concatenate([jnp.cos(angles), jnp.sin(angles)], 1)
    here = lax.dynamic_index_in_dim(turns, 2 * col + row, 0, keepdims=False)
    own_stripes = 2 * jnp.arange(cols, dtype=jnp.int32) + row
    own_places = own_stripes[:, None] * width + lane[None]
    starts = piece_starts[0]
    inside = (own_places[..., None] >= starts) & (own_places[..., None] < starts + PIECE)
    limit = jnp.max(jnp.where(inside, starts + PIECE - 1, own_places[..., None]), -1)
    scalars = jnp.concatenate(
        [jnp.stack([row, col, core]), jnp.max(limit, 1) // KEYS + 1]
    ).astype(jnp.int32)
    limit = limit[:, None, :]

    soon = gather_halves(blocks[0], order)
    next(soon)
    next(soon)
    late = gather_halves(order.next(blocks[1]), order)
    next(late)
    soon = next(soon)
    next(late)
    rest = lax.all_gather(order.next(rest), ("dp", "row", "col"), axis=0, tiled=False)
    rest = rest.reshape((-1, 2, cols) + rest.shape[1:])[:SLICES]
    w_groups, own = [], []

    def begin(group, source):
        low, high = groups[group]
        weight, pieces = project(order.next(scalars), h_one, here, source, high - low)
        order.done(weight)
        w_groups.append(weight)
        pieces = col_trade(pieces)
        own.extend((pieces, 3 * HEAD * i) for i in range(high - low))

    begin(0, soon)
    begin(1, next(late))
    g = half_rows(after(cotangent, own[-1][0]))
    forward, other = [], [None] * slots
    earlier = ()

    def share(slot):
        packed = pack(order.next(scalars), *own[slot])
        order.done(packed)
        other[slot] = row_swap(packed)

    share(0)
    for slot in range(slots):
        results = attend(order.next(scalars), *own[slot], other[slot], limit, earlier if slot < slots - 1 else ())
        order.done(results[2])
        forward.append(results)
        if slot < slots - 1:
            earlier = (results[0],)
        if slot == 0:
            for later in range(1, slots):
                share(later)
    first = col_trade(forward[slots - 2][0])
    last = col_trade(forward[slots - 1][0])

    kept = middle(order.next(scalars), x, g, small, first, last, rest, slots)
    (
        block_own,
        block_other,
        d_middle,
        h_two,
        d_branch,
        d_attended,
        active,
        d_hidden,
        mixed,
        sums,
        d_first,
        d_last,
    ) = kept
    order.done(d_middle)

    d_last = col_trade(d_last)
    grads = weight_grads(order.next(scalars), h_two, d_branch, d_attended, active, d_hidden, mixed, slots)
    order.done(grads)
    extra = lax.axis_size("dp") - SLICES
    grads = jnp.pad(grads, ((0, extra),) + ((0, 0),) * 4) if extra else grads
    grads = lax.psum_scatter(
        grads.reshape((-1,) + grads.shape[3:]), ("dp", "row", "col"), scatter_dimension=0, tiled=True
    )
    d_first = col_trade(d_first)

    back, shared = {}, {}

    def pull(slot):
        grad = (d_last, 0) if slot == slots - 1 else (d_first, slot * HEAD)
        d_query, d_own, d_other = attend_back(
            order.next(scalars), *own[slot], other[slot], *grad, *forward[slot][1:], limit, turns
        )
        order.done(d_other)
        shared[slot] = d_query, d_own, row_swap(d_other)

    def send(slot):
        pieces = merge(order.next(scalars), *shared[slot])
        order.done(pieces)
        back[slot] = col_trade(pieces)

    d_hs = []

    def finish(group):
        low, high = groups[group]
        pieces = [back[slot] for slot in range(low, high)]
        d_h, mine, theirs = unproject(order.next(scalars), h_one, w_groups[group], pieces)
        order.done(d_h)
        d_hs.append(d_h)
        steps = scatter_halves(mine, theirs, order)
        next(steps)
        return steps

    for slot in reversed(range(slots)):
        pull(slot)
        if slot < slots - 1:
            send(slot + 1)
    send(0)
    late = finish(1)
    next(late)
    soon = finish(0)
    d_h_one = d_hs[0] + d_hs[1]
    normed = centered * inv_std
    scaled = d_h_one * gain_one
    mean_grad = jnp.mean(scaled, -1, keepdims=True)
    mean_proj = jnp.mean(scaled * normed, -1, keepdims=True)
    d_tokens = d_middle + inv_std * (scaled - mean_grad - normed * mean_proj)
    sums = jnp.concatenate([jnp.sum(d_h_one, 0)[None], jnp.sum(d_h_one * normed, 0)[None], sums[:5]], 0)

    order.done(d_tokens, sums)

    def whole_rows(own_part, other_part):
        return jnp.concatenate(in_order(row, own_part, row_swap(other_part)), 0)

    tokens_out = whole_rows(d_tokens[:, :part], d_tokens[:, part:])
    block_out = whole_rows(block_own, block_other)

    next(soon)
    next(late)
    next(soon)
    next(late)
    next(soon)
    late, soon = next(late), next(soon)
    d_qkv = []
    for (low, high), found in zip(groups, (soon, late)):
        parts = [half.reshape(high - low, -1, part) for half in found]
        d_qkv.append(jnp.concatenate(parts, 1).reshape(-1, part))
    d_qkv = jnp.concatenate(d_qkv, 0)

    grads = lax.all_gather(grads[0], "dp", axis=0, tiled=False)[:SLICES].astype(f32)
    rows = slots * HEAD // SLICES
    step = part // 2
    ordered = [grads[2 * y + c] for c in range(2) for y in range(2)]
    d_out_proj = jnp.concatenate([each[:rows] for each in ordered], 0)
    d_down = jnp.concatenate([each[rows : rows + step] for each in ordered], 0)
    d_up = jnp.concatenate(
        [
            jnp.concatenate([grads[2 * y + c, rows + step : rows + 2 * step] for c in range(2)], 1)
            for y in range(2)
        ],
        0,
    )
    d_bias = jnp.concatenate([grads[c, rows + 2 * step] for c in range(2)], 0)

    sums = sums[:, :part] + row_swap(sums[:, part:])
    for bit in range(bits("col")):
        sums = sums + col_swap(sums, bit)
    per_seq = jnp.concatenate(
        [
            sums[0:1],
            sums[1:2] * gain_attn,
            sums[2:4],
            sums[4:5] * gain_mlp,
            sums[5:6],
            sums[1:2] * (1.0 + modulation[1]),
            sums[4:5] * (1.0 + modulation[4]),
            sums[6:7],
            jnp.pad(condition, (0, part - COND))[None],
        ],
        0,
    )[None]
    for bit in range(bits("dp")):
        per_seq = jnp.concatenate(in_order(dp_bit(bit), per_seq, dp_swap(per_seq, bit)), 0)
    conditions = per_seq[:, SMALL, :COND]
    d_mod_w = sum(conditions[s][:, None, None] * per_seq[s, :6][None] for s in range(per_seq.shape[0]))
    totals = jnp.sum(per_seq[:, :SMALL], 0)

    return (
        block_out,
        tokens_out,
        d_mod_w,
        totals[:6],
        totals[6],
        d_qkv,
        d_out_proj,
        totals[7],
        d_up,
        d_bias,
        d_down,
        totals[8],
    )


def solution(mesh):
    blocks = P(("dp", "col"), "row")
    return jax.shard_map(
        shards,
        mesh=mesh,
        in_specs=(
            blocks,
            blocks,
            P("dp"),
            P("dp", None),
            P(None, None, "row"),
            P(None, "row"),
            P("row"),
            P("col", "row"),
            P("col", "row"),
            P("row"),
            P("row", "col"),
            P("col"),
            P("col", "row"),
            P("row"),
        ),
        out_specs=(
            blocks,
            blocks,
            P(None, None, "row"),
            P(None, "row"),
            P("row"),
            P("col", "row"),
            P("col", "row"),
            P("row"),
            P("row", "col"),
            P("col"),
            P("col", "row"),
            P("row"),
        ),
        check_vma=False,
    )
```

```python
import functools
import math

import jax
import jax.numpy as jnp
from jax import lax
from jax.experimental import pallas as pl
from jax.experimental.pallas import tpu as pltpu
from jax.sharding import PartitionSpec as P

D = 768
HEAD = 64
HALF = HEAD // 2
COND = 128
PIECE = 256
KEYS = 256
LANES = 128
PAD = 16
CHUNK = 128
SLICES = 4
SCORE = HEAD ** (-0.5) * math.log2(math.e)
MASKED = -1e30

precise = lax.Precision.HIGHEST
epsilon = 1e-05
f32 = jnp.float32
bf16 = jnp.bfloat16


def row_swap(value):
    return lax.ppermute(value, "row", [(0, 1), (1, 0)])


def dp_swap(value, bit):
    return lax.ppermute(value, "dp", [(i, i ^ (1 << bit)) for i in range(lax.axis_size("dp"))])


def pair_moves(hop):
    moves = []
    for source in range(lax.axis_size("dp")):
        for x in range(2):
            target = (source & ~1) | (x ^ hop)
            moves.append((2 * source + x, 2 * target + (source & 1)))
    return moves


def pair_to(first, second):
    return [lax.ppermute(v, ("dp", "row"), pair_moves(hop)) for hop, v in enumerate((first, second))]


def pair_from(first, second):
    return [
        lax.ppermute(v, ("dp", "row"), [(b, a) for a, b in pair_moves(hop)])
        for hop, v in enumerate((first, second))
    ]


def col_swap(value, bit):
    return lax.ppermute(value, "col", [(i, i ^ (1 << bit)) for i in range(lax.axis_size("col"))])


def col_from(value, hop):
    size = lax.axis_size("col")
    return lax.ppermute(value, "col", [(i, (i + hop) % size) for i in range(size)]) if hop else value


def col_trade(value):
    return lax.all_to_all(value, "col", 0, 0, tiled=True)


def bits(axis):
    return lax.axis_size(axis).bit_length() - 1


def dp_bit(bit):
    return (lax.axis_index("dp") >> bit) % 2


def in_order(bit, mine, theirs):
    first = bit == 0
    return jnp.where(first, mine, theirs), jnp.where(first, theirs, mine)


def half_at(value, index, axis):
    size = value.shape[axis] // 2
    return lax.dynamic_slice_in_dim(value, index * size, size, axis)


def gather_halves(mine, order):
    pieces = [col_from(mine, k) for k in range(lax.axis_size("col"))]
    yield
    own = jnp.stack(order.next(pieces))
    order.done(own)
    other = row_swap(own)
    own_far = dp_swap(own, 0)
    yield
    other = order.next(other)
    order.done(other)
    yield [own, other, own_far, dp_swap(other, 0)]


def scatter_halves(mine, theirs, order, hops):
    def added(first, second):
        return (first.astype(f32) + second.astype(f32)).astype(bf16)

    heard = dp_swap(theirs, 0)
    yield
    heard = order.next(heard)
    keep, other = added(mine[0], heard[0]), added(mine[1], heard[1])
    order.done(keep, other)
    heard = row_swap(other)
    yield
    total = added(keep, order.next(heard))
    order.done(total)
    if hops:
        size, col = lax.axis_size("col"), lax.axis_index("col")
        parts = jnp.stack([col_from(total[lax.rem(col + k, size)], k) for k in range(size)])
    else:
        parts = col_trade(total)
    yield
    total = jnp.sum(order.next(parts).astype(f32), 0)
    order.done(total)
    for bit in range(1, bits("dp")):
        total = total + dp_swap(total, bit)
    yield
    yield in_order(dp_bit(0), total, dp_swap(total, 0))


def after(value, *others):
    return lax.optimization_barrier((value, others))[0]


class Order:
    def __init__(self):
        self.last = ()

    def next(self, value):
        return after(value, self.last)

    def done(self, *results):
        self.last = results


def contract(first, second, first_axis, second_axis):
    return lax.dot_general(
        first, second, (((first_axis,), (second_axis,)), ((), ())), preferred_element_type=f32
    )


def turned(vectors):
    return vectors.astype(f32).T.astype(bf16)


def in_vmem(count):
    return [pl.BlockSpec(memory_space=pltpu.VMEM)] * count


def in_place(count):
    return [pl.BlockSpec(memory_space=pl.ANY)] * count


SCALARS = pl.BlockSpec(memory_space=pltpu.SMEM)


def like(shape, dtype):
    return jax.ShapeDtypeStruct(shape, dtype)


def cost(flops, moved, powers=0):
    return pl.CostEstimate(flops=flops, bytes_accessed=moved, transcendentals=powers)


def project_kernel(count, slots, scalars, h_ref, turn_ref, *refs):
    sources, w_ref, out_ref, sems = refs[:4], refs[4], refs[5], refs[6]
    part = sources[0].shape[2]
    rows = 3 * HALF
    copies = []
    for index, source in enumerate(sources):
        o, core = index % 2, index // 2
        place = scalars[2] ^ core
        for k in range(count):
            column = lax.rem(scalars[1] + count - k, count)
            for s in range(slots):
                start = pl.multiple_of(column * 3 * HEAD + place * rows, PAD)
                copies.append(
                    pltpu.make_async_copy(
                        source.at[k, pl.ds(s * rows, rows), :],
                        w_ref.at[s, pl.ds(start, rows), pl.ds(o * part, part)],
                        sems.at[len(copies)],
                    )
                )
    for copy in copies:
        copy.start()
    for copy in copies:
        copy.wait()
    h = h_ref[...]
    cosine, sine = turn_ref[0:HALF, :], turn_ref[HALF:HEAD, :]
    for s in range(slots):
        base = s * 3 * HEAD
        for k in range(count):
            values = contract(w_ref[s, k * 3 * HEAD : (k + 1) * 3 * HEAD, :], h, 1, 1)
            for i in range(2):
                low, middle, high = i * HEAD, i * HEAD + HALF, (i + 1) * HEAD
                first, second = values[low:middle], values[middle:high]
                out_ref[k, base + low : base + middle, :] = (first * cosine - second * sine).astype(bf16)
                out_ref[k, base + middle : base + high, :] = (second * cosine + first * sine).astype(bf16)
            out_ref[k, base + 2 * HEAD : base + 3 * HEAD, :] = values[2 * HEAD :].astype(bf16)


def project(scalars, h, turn, sources, slots):
    count, _, part = sources[0].shape
    width = h.shape[0]
    return pl.pallas_call(
        functools.partial(project_kernel, count, slots),
        in_specs=[SCALARS] + in_vmem(2) + in_place(len(sources)),
        out_specs=in_vmem(2),
        out_shape=[
            like((slots, count * 3 * HEAD, 2 * part), bf16),
            like((count, slots * 3 * HEAD, width), bf16),
        ],
        scratch_shapes=[pltpu.SemaphoreType.DMA((len(sources) * count * slots,))],
        cost_estimate=cost(slots * 2 * count * 3 * HEAD * 2 * part * width, 3_000_000 * slots),
        name="project",
    )(scalars, h, turn, *sources)


def pack_kernel(offset, _, own_ref, out_ref):
    for index in range(own_ref.shape[0]):
        out_ref[index] = own_ref[index, offset + HEAD : offset + 3 * HEAD, :]


def pack(scalars, own, offset):
    count, _, width = own.shape
    return pl.pallas_call(
        functools.partial(pack_kernel, offset),
        in_specs=[SCALARS] + in_vmem(1),
        out_specs=in_vmem(1)[0],
        out_shape=like((count, 2 * HEAD, width), bf16),
        cost_estimate=cost(1000, 1_000_000),
        name="pack",
    )(scalars, own)


def merge_kernel(_, d_query_ref, d_own_ref, heard_ref, out_ref):
    for index in range(out_ref.shape[0]):
        out_ref[index, :HEAD, :] = d_query_ref[index]
        out_ref[index, HEAD:, :] = (d_own_ref[index] + heard_ref[index].astype(f32)).astype(bf16)


def merge(scalars, d_query, d_own, heard):
    count, _, width = d_query.shape
    return pl.pallas_call(
        merge_kernel,
        in_specs=[SCALARS] + in_vmem(3),
        out_specs=in_vmem(1)[0],
        out_shape=like((count, 3 * HEAD, width), bf16),
        cost_estimate=cost(1000, 2_000_000),
        name="merge",
    )(scalars, d_query, d_own, heard)


def place_stripes(scalars, own_ref, offset, other_ref, keys, values_t, keys_t=None, values=None):
    side = scalars[2]
    count, _, width = own_ref.shape
    parts = width // LANES
    for place in range(count):
        for stripe, ref, base in (
            (2 * place + side, own_ref.at[place], offset + HEAD),
            (2 * place + 1 - side, other_ref.at[place], 0),
        ):
            start = pl.multiple_of(stripe * width, LANES)
            key_t = ref[base : base + HEAD, :]
            value_t = ref[base + HEAD : base + 2 * HEAD, :]
            keys[pl.ds(start, width), :] = turned(key_t)
            if values is not None:
                values[pl.ds(start, width), :] = turned(value_t)
            for part in range(parts):
                lanes = slice(part * LANES, (part + 1) * LANES)
                if values_t is not None:
                    values_t[stripe * parts + part] = value_t[:, lanes]
                if keys_t is not None:
                    keys_t[stripe * parts + part] = key_t[:, lanes]


def lane_block(ref, block):
    parts = KEYS // LANES
    return jnp.concatenate([ref[block * parts + part] for part in range(parts)], 1)


def attend_kernel(offset, earlier, scalars, own_ref, other_ref, limit_ref, *refs):
    before_ref, (out_ref, wide_ref, log_ref, keys, values_t) = refs[:earlier], refs[earlier:]
    count, _, width = own_ref.shape
    place_stripes(scalars, own_ref, offset, other_ref, keys, values_t)
    side = scalars[2]

    def stripe(place, _):
        query_t = own_ref[place, offset : offset + HEAD, :]
        limit = limit_ref[place]
        first = (2 * place + side) * width

        def step(masked, block, carry):
            top, total, mixed = carry
            start = pl.multiple_of(block * KEYS, KEYS)
            scores = jnp.dot(keys[pl.ds(start, KEYS), :], query_t, preferred_element_type=f32) * SCORE
            if masked:
                key = start + lax.broadcasted_iota(jnp.int32, scores.shape, 0)
                scores = jnp.where(key <= limit, scores, MASKED)
            new_top = jnp.maximum(top, jnp.max(scores, 0, keepdims=True))
            fade = jnp.exp2(top - new_top)
            weight = jnp.exp2(scores - new_top)
            total = total * fade + jnp.sum(weight, 0, keepdims=True)
            mixed = mixed * fade + jnp.dot(
                lane_block(values_t, block), weight.astype(bf16), preferred_element_type=f32
            )
            return new_top, total, mixed

        carry = (
            jnp.full((1, width), MASKED, f32),
            jnp.zeros((1, width), f32),
            jnp.zeros((HEAD, width), f32),
        )
        whole = first // KEYS
        carry = lax.fori_loop(0, whole, functools.partial(step, False), carry)
        top, total, mixed = lax.fori_loop(whole, scalars[3 + place], functools.partial(step, True), carry)
        mixed = mixed / total
        wide_ref[place] = mixed
        log_ref[place] = top + jnp.log2(total)
        return 0

    lax.fori_loop(0, count, stripe, 0)
    rows = out_ref.shape[1]
    for place in range(count):
        out_ref[place, rows - HEAD :, :] = wide_ref[place].astype(bf16)
        if earlier:
            out_ref[place, : rows - HEAD, :] = before_ref[0][place]


def attend(scalars, own, offset, other, limit, earlier):
    count, _, width = own.shape
    seq_len = 2 * count * width
    rows = HEAD + (earlier[0].shape[1] if earlier else 0)
    return pl.pallas_call(
        functools.partial(attend_kernel, offset, len(earlier)),
        in_specs=[SCALARS] + in_vmem(3 + len(earlier)),
        out_specs=in_vmem(3),
        out_shape=[
            like((count, rows, width), bf16),
            like((count, HEAD, width), f32),
            like((count, 1, width), f32),
        ],
        scratch_shapes=[
            pltpu.VMEM((seq_len, HEAD), bf16),
            pltpu.VMEM((seq_len // LANES, HEAD, LANES), bf16),
        ],
        cost_estimate=cost(8_000_000_000, 3_000_000, 3_000_000),
        name="attend",
    )(scalars, own, other, limit, *earlier)


def attend_back_kernel(
    offset,
    grad_offset,
    scalars,
    own_ref,
    other_ref,
    grad_ref,
    wide_ref,
    log_ref,
    limit_ref,
    turn_ref,
    d_query_ref,
    d_own_ref,
    d_other_ref,
    keys,
    values,
    keys_t,
    d_keys,
    d_values,
):
    count, _, width = own_ref.shape
    place_stripes(scalars, own_ref, offset, other_ref, keys, None, keys_t, values)
    side = scalars[2]
    d_keys[...] = jnp.zeros_like(d_keys)
    d_values[...] = jnp.zeros_like(d_values)

    def turn_back(vectors, stripe):
        cosine, sine = turn_ref[stripe, 0:HALF, :], turn_ref[stripe, HALF:HEAD, :]
        upper, lower = vectors[0:HALF], vectors[HALF:HEAD]
        return jnp.concatenate([upper * cosine + lower * sine, lower * cosine - upper * sine], 0)

    def of_stripe(place, _):
        query_t = own_ref[place, offset : offset + HEAD, :]
        grad_t = grad_ref[place, grad_offset : grad_offset + HEAD, :]
        query = turned(query_t)
        grad = turned(grad_t)
        drift = jnp.sum(grad_t.astype(f32) * wide_ref[place], 0, keepdims=True)
        log_sum = log_ref[place]
        limit = limit_ref[place]
        stripe = 2 * place + side

        def step(masked, block, d_query):
            start = pl.multiple_of(block * KEYS, KEYS)
            rows = pl.ds(start, KEYS)
            scores = jnp.dot(keys[rows, :], query_t, preferred_element_type=f32) * SCORE
            weight = jnp.exp2(scores - log_sum)
            if masked:
                key = start + lax.broadcasted_iota(jnp.int32, scores.shape, 0)
                weight = jnp.where(key <= limit, weight, 0.0)
            d_weight = jnp.dot(values[rows, :], grad_t, preferred_element_type=f32)
            d_scores = (weight * (d_weight - drift)).astype(bf16)
            d_values[rows, :] += jnp.dot(weight.astype(bf16), grad, preferred_element_type=f32)
            d_keys[rows, :] += jnp.dot(d_scores, query, preferred_element_type=f32)
            return d_query + jnp.dot(lane_block(keys_t, block), d_scores, preferred_element_type=f32)

        d_query = jnp.zeros((HEAD, width), f32)
        whole = stripe * width // KEYS
        d_query = lax.fori_loop(0, whole, functools.partial(step, False), d_query)
        d_query = lax.fori_loop(whole, scalars[3 + place], functools.partial(step, True), d_query)
        d_query_ref[place] = turn_back(d_query * HEAD ** (-0.5), stripe).astype(bf16)
        return 0

    lax.fori_loop(0, count, of_stripe, 0)

    def finish(place, _):
        for stripe, ref in ((2 * place + side, d_own_ref), (2 * place + 1 - side, d_other_ref)):
            start = pl.multiple_of(stripe * width, LANES)
            d_key = d_keys[pl.ds(start, width), :].T * HEAD ** (-0.5)
            ref[place, 0:HEAD, :] = turn_back(d_key, stripe).astype(ref.dtype)
            ref[place, HEAD : 2 * HEAD, :] = d_values[pl.ds(start, width), :].T.astype(ref.dtype)
        return 0

    lax.fori_loop(0, count, finish, 0)


def attend_back(scalars, own, offset, other, grad, grad_offset, wide, log_sum, limit, turns):
    count, _, width = own.shape
    seq_len = 2 * count * width
    return pl.pallas_call(
        functools.partial(attend_back_kernel, offset, grad_offset),
        in_specs=[SCALARS] + in_vmem(7),
        out_specs=in_vmem(3),
        out_shape=[
            like((count, HEAD, width), bf16),
            like((count, 2 * HEAD, width), f32),
            like((count, 2 * HEAD, width), bf16),
        ],
        scratch_shapes=[
            pltpu.VMEM((seq_len, HEAD), bf16),
            pltpu.VMEM((seq_len, HEAD), bf16),
            pltpu.VMEM((seq_len // LANES, HEAD, LANES), bf16),
            pltpu.VMEM((seq_len, HEAD), f32),
            pltpu.VMEM((seq_len, HEAD), f32),
        ],
        cost_estimate=cost(16_000_000_000, 4_000_000, 3_000_000),
        name="attend_back",
    )(scalars, own, other, grad, wide, log_sum, limit, turns)


SMALL = 9
SHIFT_A, SCALE_A, GATE_A, SHIFT_M, SCALE_M, GATE_M, GAIN_A, GAIN_M, BIAS_DOWN = range(SMALL)


def middle_kernel(slots, scalars, x_own, x_other, g_own, g_other, small_ref, first_ref, last_ref, source, *refs):
    block_own, block_other, d_middle_ref, h_ref, df_ref, d_att_ref, active_ref, d_hidden_ref, mixed_ref, sums_ref = refs[:10]
    d_first, d_last, w_out, up, down, bias, attended_ref, mid_ref, f_ref, dh_ref, sems = refs[10:]
    width, part = x_own.shape
    count = first_ref.shape[0]
    out_rows = slots * HEAD // SLICES
    step_rows = part // 2
    copies = {"out": [], "up": [], "down": [], "bias": []}
    used = 0

    def copy(kind, origin, target):
        nonlocal used
        copies[kind].append(pltpu.make_async_copy(origin, target, sems.at[used]))
        used += 1

    for index in range(SLICES):
        y, core = index // 2, index % 2
        for o in range(2):
            lanes = pl.ds(o * part, part)
            for k in range(count):
                b = core * count + k
                origin = source.at[index, scalars[0] ^ o, k]
                start = k * slots * HEAD + (2 * core + y) * out_rows
                copy("out", origin.at[pl.ds(0, out_rows), :], w_out.at[pl.ds(start, out_rows), lanes])
                start = y * step_rows
                copy("down", origin.at[pl.ds(out_rows, step_rows), :], down.at[b, pl.ds(start, step_rows), lanes])
                copy(
                    "up",
                    origin.at[pl.ds(out_rows + step_rows, step_rows), :],
                    up.at[b, pl.ds(o * part + start, step_rows), :],
                )
                if o == 0 and y == 0:
                    copy("bias", origin.at[pl.ds(out_rows + 2 * step_rows, PAD), :], bias.at[b])
    for kind in copies:
        for each in copies[kind]:
            each.start()
    for k in range(count):
        base = k * slots * HEAD
        mixed_ref[base : base + (slots - 1) * HEAD, :] = first_ref[k]
        mixed_ref[base + (slots - 1) * HEAD : base + slots * HEAD, :] = last_ref[k]

    def small(index):
        return small_ref[index : index + 1, :]

    def wide_rows(own, other, rows):
        return jnp.concatenate([own[rows, :].astype(f32), other[rows, :].astype(f32)], 1)

    def norm(values, rows):
        mean = jnp.mean(values, 1, keepdims=True)
        centered = values - mean
        inv_std = lax.rsqrt(jnp.mean(centered * centered, 1, keepdims=True) + epsilon)
        return centered * inv_std, inv_std

    for each in copies["out"]:
        each.wait()
    attended_ref[...] = contract(mixed_ref[...], w_out[...], 0, 0)
    f_ref[...] = jnp.zeros_like(f_ref)
    dh_ref[...] = jnp.zeros_like(dh_ref)
    sums_ref[...] = jnp.zeros_like(sums_ref)

    def before(index, _):
        rows = pl.ds(pl.multiple_of(index * CHUNK, CHUNK), CHUNK)
        middle = wide_rows(x_own, x_other, rows) + small(GATE_A) * attended_ref[rows, :]
        mid_ref[rows, :] = middle
        normed, _ = norm(middle, rows)
        h_ref[rows, :] = (normed * (small(GAIN_M) * (1.0 + small(SCALE_M))) + small(SHIFT_M)).astype(bf16)
        df_ref[rows, :] = (wide_rows(g_own, g_other, rows) * small(GATE_M)).astype(bf16)
        return 0

    lax.fori_loop(0, width // CHUNK, before, 0)
    for kind in ("up", "down", "bias"):
        for each in copies[kind]:
            each.wait()

    def feed(b, _):
        h, df = h_ref[...], df_ref[...]
        u = contract(h, up[b], 1, 0) + bias[b][0:1, :].astype(f32)
        squared = u * u
        bent = jnp.tanh(0.79788456 * u * (1.0 + 0.044715 * squared))
        active = (0.5 * u * (1.0 + bent)).astype(bf16)
        slope = 0.5 * (1.0 + bent) + 0.5 * u * (1.0 - bent * bent) * (
            0.79788456 * (1.0 + 3.0 * 0.044715 * squared)
        )
        active_ref[b] = active
        d_hidden = (slope * contract(df, down[b], 1, 1)).astype(bf16)
        d_hidden_ref[b] = d_hidden
        f_ref[...] += contract(active, down[b], 1, 0)
        dh_ref[...] += contract(d_hidden, up[b], 1, 1)
        return 0

    lax.fori_loop(0, 2 * count, feed, 0)

    def after(index, _):
        rows = pl.ds(pl.multiple_of(index * CHUNK, CHUNK), CHUNK)
        middle = mid_ref[rows, :]
        branch = f_ref[rows, :] + small(BIAS_DOWN)
        out = (middle + small(GATE_M) * branch).astype(bf16)
        block_own[rows, :] = out[:, :part]
        block_other[rows, :] = out[:, part:]
        upstream = wide_rows(g_own, g_other, rows)
        normed, inv_std = norm(middle, rows)
        dh = dh_ref[rows, :]
        scaled = dh * (small(GAIN_M) * (1.0 + small(SCALE_M)))
        mean_grad = jnp.mean(scaled, 1, keepdims=True)
        mean_proj = jnp.mean(scaled * normed, 1, keepdims=True)
        d_middle = upstream + inv_std * (scaled - mean_grad - normed * mean_proj)
        d_middle_ref[rows, :] = d_middle
        d_att_ref[rows, :] = (d_middle * small(GATE_A)).astype(bf16)
        for i, value in enumerate(
            (d_middle * attended_ref[rows, :], dh, dh * normed, upstream * branch, df_ref[rows, :].astype(f32))
        ):
            sums_ref[i : i + 1, :] += jnp.sum(value, 0, keepdims=True)
        return 0

    lax.fori_loop(0, width // CHUNK, after, 0)
    d_att = d_att_ref[...]
    for k in range(count):
        base = k * slots * HEAD
        values = contract(w_out[base : base + slots * HEAD, :], d_att, 1, 1).astype(bf16)
        d_first[k] = values[: (slots - 1) * HEAD]
        d_last[k] = values[(slots - 1) * HEAD :]


def middle(scalars, x, g, small, first, last, source, slots):
    count = first.shape[0]
    width, part = x[0].shape
    blocks = 2 * count
    heads = count * slots * HEAD
    return pl.pallas_call(
        functools.partial(middle_kernel, slots),
        in_specs=[SCALARS] + in_vmem(7) + in_place(1),
        out_specs=in_vmem(12),
        out_shape=[
            like((width, part), bf16),
            like((width, part), bf16),
            like((width, 2 * part), f32),
            like((width, 2 * part), bf16),
            like((width, 2 * part), bf16),
            like((width, 2 * part), bf16),
            like((blocks, width, part), bf16),
            like((blocks, width, part), bf16),
            like((heads, width), bf16),
            like((8, 2 * part), f32),
            like((count, (slots - 1) * HEAD, width), bf16),
            like((count, HEAD, width), bf16),
        ],
        scratch_shapes=[
            pltpu.VMEM((heads, 2 * part), bf16),
            pltpu.VMEM((blocks, 2 * part, part), bf16),
            pltpu.VMEM((blocks, part, 2 * part), bf16),
            pltpu.VMEM((blocks, PAD, part), bf16),
            pltpu.VMEM((width, 2 * part), f32),
            pltpu.VMEM((width, 2 * part), f32),
            pltpu.VMEM((width, 2 * part), f32),
            pltpu.VMEM((width, 2 * part), f32),
            pltpu.SemaphoreType.DMA(((6 * SLICES + 2) * count,)),
        ],
        cost_estimate=cost(2 * width * (4 * blocks * part * 2 * part + 2 * heads * 2 * part), 14_000_000, 2_000_000),
        name="middle",
    )(scalars, *x, *g, small, first, last, source)


def grads_kernel(slots, scalars, h_ref, df_ref, d_att_ref, active_ref, d_hidden_ref, mixed_ref, out_ref, d_out):
    part = h_ref.shape[1] // 2
    count = active_ref.shape[0] // 2
    out_rows = slots * HEAD // SLICES
    step_rows = part // 2
    d_out[...] = contract(mixed_ref[...], d_att_ref[...], 1, 0).astype(bf16)

    def of_block(b, _):
        core, k = b // count, b % count
        d_hidden = d_hidden_ref[b]
        d_up = contract(h_ref[...], d_hidden, 0, 0).astype(bf16)
        d_down = contract(active_ref[b], df_ref[...], 0, 0).astype(bf16)
        d_bias = jnp.broadcast_to(jnp.sum(d_hidden.astype(f32), 0, keepdims=True), (PAD, part)).astype(bf16)
        for y in range(2):
            start = pl.multiple_of(k * slots * HEAD + (2 * core + y) * out_rows, PAD)
            out_part = d_out[pl.ds(start, out_rows), :]
            for o in range(2):
                target = out_ref.at[2 * y + core, scalars[0] ^ o, k]
                lanes = slice(o * part, (o + 1) * part)
                start = o * part + y * step_rows
                target[:out_rows, :] = out_part[:, lanes]
                target[out_rows : out_rows + step_rows, :] = d_down[y * step_rows : (y + 1) * step_rows, lanes]
                target[out_rows + step_rows : out_rows + 2 * step_rows, :] = d_up[start : start + step_rows]
                target[out_rows + 2 * step_rows :, :] = d_bias
        return 0

    lax.fori_loop(0, 2 * count, of_block, 0)


def weight_grads(scalars, h, df, d_att, active, d_hidden, mixed, slots):
    count = active.shape[0] // 2
    width, whole = h.shape
    part = whole // 2
    return pl.pallas_call(
        functools.partial(grads_kernel, slots),
        in_specs=[SCALARS] + in_vmem(6),
        out_specs=in_vmem(1)[0],
        out_shape=like((SLICES, 2, count, slots * HEAD // SLICES + part + PAD, part), bf16),
        scratch_shapes=[pltpu.VMEM((mixed.shape[0], whole), bf16)],
        cost_estimate=cost(2 * width * (4 * count * part * whole + mixed.shape[0] * whole), 20_000_000),
        name="weight_grads",
    )(scalars, h, df, d_att, active, d_hidden, mixed)


def unproject_kernel(scalars, h_ref, w_ref, *refs):
    slots = w_ref.shape[0]
    pieces, (dh_ref, mine, theirs, grad) = refs[:slots], refs[slots:]
    count, rows, width = pieces[0].shape
    part = h_ref.shape[1] // 2
    half = rows // 2
    dh = jnp.zeros(dh_ref.shape, f32)
    for s in range(slots):
        back = pieces[s][...].reshape(count * rows, width)
        dh = dh + contract(back, w_ref[s], 0, 0)
        grad[...] = contract(back, h_ref[...], 1, 0).astype(bf16)
        for core, target in enumerate((mine, theirs)):
            place = scalars[2] ^ core
            for k in range(count):
                start = pl.multiple_of(k * rows + place * half, PAD)
                values = grad[pl.ds(start, half), :]
                for o in range(2):
                    target[o, k, s * half : (s + 1) * half, :] = values[:, o * part : (o + 1) * part]
    dh_ref[...] = dh


def unproject(scalars, h, weight, pieces):
    width, whole = h.shape
    slots = len(pieces)
    count = pieces[0].shape[0]
    shape = like((2, count, slots * 3 * HALF, whole // 2), bf16)
    return pl.pallas_call(
        unproject_kernel,
        in_specs=[SCALARS] + in_vmem(2 + slots),
        out_specs=in_vmem(3),
        out_shape=[like((width, whole), f32), shape, shape],
        scratch_shapes=[pltpu.VMEM((weight.shape[1], whole), bf16)],
        cost_estimate=cost(slots * 4 * width * whole * weight.shape[1], 5_000_000 * slots),
        name="unproject",
    )(scalars, h, weight, *pieces)


def embed_time(time_step):
    half_size = COND // 2
    frequency = jnp.exp(-math.log(10000.0) * jnp.arange(half_size, dtype=f32) / half_size)
    angles = time_step * frequency
    return jax.nn.silu(jnp.concatenate([jnp.cos(angles), jnp.sin(angles)]))


def shards(
    tokens, cotangent, timestep, piece_starts, w_mod, b_mod, gain_attn, w_qkv, w_out, gain_mlp, w_up, b_up, w_down, b_down
):
    cols = lax.axis_size("col")
    row, col, core, far = lax.axis_index("row"), lax.axis_index("col"), dp_bit(0), dp_bit(1)
    block_rows, part = tokens.shape
    width = block_rows // 2
    slots = w_qkv.shape[0] // (3 * HEAD)

    def relative(heard):
        return in_order(core ^ row, *heard)

    def half_rows(block):
        return relative(pair_to(half_at(block, row, 0), half_at(block, 1 - row, 0)))

    x = half_rows(tokens)

    order = Order()

    w_parts = w_qkv.reshape(slots, 3 * HEAD, part)
    groups = [(0, 1), (1, slots)]
    blocks = [half_at(w_parts[low:high], core, 1).reshape(-1, part) for low, high in groups]

    def quarter_at(block):
        return half_at(half_at(block, core, 0), far, 0)

    bias = jnp.broadcast_to(half_at(b_up[None], core, 1), (PAD, part))
    rest = jnp.concatenate(
        [quarter_at(w_out), quarter_at(w_down), half_at(half_at(w_up, core, 1), far, 0), bias], 0
    )

    condition = embed_time(timestep[0].astype(f32))
    modulation = jnp.einsum("k,kjd->jd", condition, w_mod.astype(f32), precision=precise) + b_mod
    known = jnp.concatenate([condition, piece_starts[0].astype(f32)])
    known = jnp.pad(known, (0, part - known.shape[0]))
    small = jnp.concatenate([modulation, gain_attn[None], gain_mlp[None], b_down[None], known[None]], 0)
    small = jnp.concatenate(relative(pair_to(small, small)), 1)
    condition = small[SMALL, :COND]
    starts = small[SMALL, COND : COND + piece_starts.shape[1]].astype(jnp.int32)

    residual = jnp.concatenate(x, 1).astype(f32)
    centered = residual - jnp.mean(residual, -1, keepdims=True)
    inv_std = lax.rsqrt(jnp.mean(centered * centered, -1, keepdims=True) + epsilon)
    gain_one = small[GAIN_A] * (1.0 + small[SCALE_A])
    h_one = (centered * inv_std * gain_one + small[SHIFT_A]).astype(bf16)

    lane = jnp.arange(width, dtype=jnp.int32)
    frequency = jnp.exp(-math.log(10000.0) * jnp.arange(HALF, dtype=f32) / HALF)
    places = jnp.arange(2 * cols, dtype=jnp.int32)[:, None] * width + lane[None]
    angles = places.astype(f32)[:, None, :] * frequency[None, :, None]
    turns = jnp.concatenate([jnp.cos(angles), jnp.sin(angles)], 1)
    here = lax.dynamic_index_in_dim(turns, 2 * col + core, 0, keepdims=False)
    own_stripes = 2 * jnp.arange(cols, dtype=jnp.int32) + core
    own_places = own_stripes[:, None] * width + lane[None]
    inside = (own_places[..., None] >= starts) & (own_places[..., None] < starts + PIECE)
    limit = jnp.max(jnp.where(inside, starts + PIECE - 1, own_places[..., None]), -1)
    scalars = jnp.concatenate(
        [jnp.stack([row, col, core]), jnp.max(limit, 1) // KEYS + 1]
    ).astype(jnp.int32)
    limit = limit[:, None, :]

    soon = gather_halves(blocks[0], order)
    next(soon)
    next(soon)
    order.done(*order.last, *x, small)
    late = gather_halves(order.next(blocks[1]), order)
    next(late)
    soon = next(soon)
    next(late)
    rest = lax.all_gather(order.next(rest), ("dp", "row", "col"), axis=0, tiled=False)
    rest = rest.reshape((-1, 2, cols) + rest.shape[1:])[:SLICES]
    w_groups, own = [], []

    def begin(group, source):
        low, high = groups[group]
        weight, pieces = project(order.next(scalars), h_one, here, source, high - low)
        order.done(weight)
        w_groups.append(weight)
        pieces = col_trade(pieces)
        own.extend((pieces, 3 * HEAD * i) for i in range(high - low))

    begin(0, soon)
    begin(1, next(late))
    g = half_rows(after(cotangent, w_groups[0]))
    forward, other = [], [None] * slots
    earlier = ()

    def share(slot):
        packed = pack(order.next(scalars), *own[slot])
        order.done(packed)
        other[slot] = dp_swap(packed, 0)

    share(0)
    for slot in range(slots):
        results = attend(order.next(scalars), *own[slot], other[slot], limit, earlier if slot < slots - 1 else ())
        order.done(results[2], *(g if slot == 1 else ()))
        forward.append(results)
        if slot < slots - 1:
            earlier = (results[0],)
        if slot == 0:
            for later in range(1, slots):
                share(later)
    first = col_trade(forward[slots - 2][0])
    last = col_trade(after(forward[slots - 1][0], first))

    kept = middle(order.next(scalars), x, g, small, first, last, rest, slots)
    (
        block_own,
        block_other,
        d_middle,
        h_two,
        d_branch,
        d_attended,
        active,
        d_hidden,
        mixed,
        sums,
        d_first,
        d_last,
    ) = kept
    order.done(d_middle)

    def whole_rows(own_part, other_part):
        return jnp.concatenate(in_order(row, *pair_from(*in_order(core ^ row, own_part, other_part))), 0)

    d_last = col_trade(d_last)
    grads = weight_grads(order.next(scalars), h_two, d_branch, d_attended, active, d_hidden, mixed, slots)
    order.done(grads)
    grads = after(grads, d_last)
    extra = lax.axis_size("dp") - SLICES
    grads = jnp.pad(grads, ((0, extra),) + ((0, 0),) * 4) if extra else grads
    grads = lax.psum_scatter(
        grads.reshape((-1,) + grads.shape[3:]), ("dp", "row", "col"), scatter_dimension=0, tiled=True
    )
    d_first = col_trade(d_first)
    block_out = whole_rows(block_own, block_other)

    back, shared = {}, {}

    def pull(slot):
        grad = (d_last, 0) if slot == slots - 1 else (d_first, slot * HEAD)
        d_query, d_own, d_other = attend_back(
            order.next(scalars), *own[slot], other[slot], *grad, *forward[slot][1:], limit, turns
        )
        order.done(d_other, *((block_out,) if slot == slots - 2 else ()))
        shared[slot] = d_query, d_own, dp_swap(d_other, 0)

    def send(slot):
        pieces = merge(order.next(scalars), *shared[slot])
        order.done(pieces)
        back[slot] = col_trade(pieces)

    d_hs = []

    def finish(group):
        low, high = groups[group]
        pieces = [back[slot] for slot in range(low, high)]
        d_h, mine, theirs = unproject(order.next(scalars), h_one, w_groups[group], pieces)
        order.done(d_h)
        d_hs.append(d_h)
        steps = scatter_halves(mine, theirs, order, group > 0)
        next(steps)
        return steps

    for slot in reversed(range(slots)):
        pull(slot)
        if slot < slots - 1:
            send(slot + 1)
    send(0)
    late = finish(1)
    next(late)
    next(late)
    soon = finish(0)
    d_h_one = d_hs[0] + d_hs[1]
    normed = centered * inv_std
    scaled = d_h_one * gain_one
    mean_grad = jnp.mean(scaled, -1, keepdims=True)
    mean_proj = jnp.mean(scaled * normed, -1, keepdims=True)
    d_tokens = d_middle + inv_std * (scaled - mean_grad - normed * mean_proj)
    sums = jnp.concatenate([jnp.sum(d_h_one, 0)[None], jnp.sum(d_h_one * normed, 0)[None], sums[:5]], 0)

    order.done(d_tokens, sums)
    next(soon)
    tokens_out = whole_rows(d_tokens[:, :part], d_tokens[:, part:])

    sums = order.next(sums)
    sums = sums + dp_swap(sums, 0)
    for bit in range(bits("col")):
        sums = sums + col_swap(sums, bit)
        order.done(sums)
        if bit == 0:
            next(soon)
            next(late)
            sums = order.next(sums)
    per_seq = jnp.concatenate(
        [
            sums[0:1],
            sums[1:2] * small[GAIN_A],
            sums[2:4],
            sums[4:5] * small[GAIN_M],
            sums[5:6],
            sums[1:2] * (1.0 + small[SCALE_A]),
            sums[4:5] * (1.0 + small[SCALE_M]),
            sums[6:7],
            jnp.tile(jnp.pad(condition, (0, part - COND)), 2)[None],
        ],
        0,
    )[None]
    per_seq = jnp.concatenate(in_order(row, per_seq[..., :part], row_swap(per_seq[..., part:])), 0)
    order.done(per_seq)
    next(soon)
    for bit in range(1, bits("dp")):
        per_seq = jnp.concatenate(in_order(dp_bit(bit), per_seq, dp_swap(per_seq, bit)), 0)
    late, soon = next(late), next(soon)
    d_qkv = []
    for (low, high), found in zip(groups, (soon, late)):
        parts = [half.reshape(high - low, -1, part) for half in found]
        d_qkv.append(jnp.concatenate(parts, 1).reshape(-1, part))
    d_qkv = jnp.concatenate(d_qkv, 0)

    grads = lax.all_gather(grads[0], "dp", axis=0, tiled=False)[:SLICES].astype(f32)
    rows = slots * HEAD // SLICES
    step = part // 2
    ordered = [grads[2 * y + c] for c in range(2) for y in range(2)]
    d_out_proj = jnp.concatenate([each[:rows] for each in ordered], 0)
    d_down = jnp.concatenate([each[rows : rows + step] for each in ordered], 0)
    d_up = jnp.concatenate(
        [
            jnp.concatenate([grads[2 * y + c, rows + step : rows + 2 * step] for c in range(2)], 1)
            for y in range(2)
        ],
        0,
    )
    d_bias = jnp.concatenate([grads[c, rows + 2 * step] for c in range(2)], 0)

    conditions = per_seq[:, SMALL, :COND]
    d_mod_w = sum(conditions[s][:, None, None] * per_seq[s, :6][None] for s in range(per_seq.shape[0]))
    totals = jnp.sum(per_seq[:, :SMALL], 0)

    return (
        block_out,
        tokens_out,
        d_mod_w,
        totals[:6],
        totals[6],
        d_qkv,
        d_out_proj,
        totals[7],
        d_up,
        d_bias,
        d_down,
        totals[8],
    )


def solution(mesh):
    blocks = P(("dp", "col"), "row")
    return jax.shard_map(
        shards,
        mesh=mesh,
        in_specs=(
            blocks,
            blocks,
            P("dp"),
            P("dp", None),
            P(None, None, "row"),
            P(None, "row"),
            P("row"),
            P("col", "row"),
            P("col", "row"),
            P("row"),
            P("row", "col"),
            P("col"),
            P("col", "row"),
            P("row"),
        ),
        out_specs=(
            blocks,
            blocks,
            P(None, None, "row"),
            P(None, "row"),
            P("row"),
            P("col", "row"),
            P("col", "row"),
            P("row"),
            P("row", "col"),
            P("col"),
            P("col", "row"),
            P("row"),
        ),
        check_vma=False,
    )
```

```python
import functools
import math

import jax
import jax.numpy as jnp
from jax import lax
from jax.experimental import pallas as pl
from jax.experimental.pallas import tpu as pltpu
from jax.sharding import PartitionSpec as P

D = 768
HEAD = 64
HALF = HEAD // 2
COND = 128
PIECE = 256
KEYS = 256
LANES = 128
PAD = 16
CHUNK = 128
SLICES = 4
SCORE = HEAD ** (-0.5) * math.log2(math.e)
MASKED = -1e30

precise = lax.Precision.HIGHEST
epsilon = 1e-05
f32 = jnp.float32
bf16 = jnp.bfloat16


def row_swap(value):
    return lax.ppermute(value, "row", [(0, 1), (1, 0)])


def dp_swap(value, bit):
    return lax.ppermute(value, "dp", [(i, i ^ (1 << bit)) for i in range(lax.axis_size("dp"))])


def pair_moves(hop):
    moves = []
    for source in range(lax.axis_size("dp")):
        for x in range(2):
            target = (source & ~1) | (x ^ hop)
            moves.append((2 * source + x, 2 * target + (source & 1)))
    return moves


def pair_to(first, second):
    return [lax.ppermute(v, ("dp", "row"), pair_moves(hop)) for hop, v in enumerate((first, second))]


def pair_from(first, second):
    return [
        lax.ppermute(v, ("dp", "row"), [(b, a) for a, b in pair_moves(hop)])
        for hop, v in enumerate((first, second))
    ]


def col_swap(value, bit):
    return lax.ppermute(value, "col", [(i, i ^ (1 << bit)) for i in range(lax.axis_size("col"))])


def col_from(value, hop):
    size = lax.axis_size("col")
    return lax.ppermute(value, "col", [(i, (i + hop) % size) for i in range(size)]) if hop else value


def col_trade(value):
    return lax.all_to_all(value, "col", 0, 0, tiled=True)


def bits(axis):
    return lax.axis_size(axis).bit_length() - 1


def dp_bit(bit):
    return (lax.axis_index("dp") >> bit) % 2


def in_order(bit, mine, theirs):
    first = bit == 0
    return jnp.where(first, mine, theirs), jnp.where(first, theirs, mine)


def half_at(value, index, axis):
    size = value.shape[axis] // 2
    return lax.dynamic_slice_in_dim(value, index * size, size, axis)


def gather_halves(mine, order):
    pieces = [col_from(mine, k) for k in range(lax.axis_size("col"))]
    yield
    own = jnp.stack(order.next(pieces))
    order.done(own)
    other = row_swap(own)
    own_far = dp_swap(own, 0)
    yield
    other = order.next(other)
    order.done(other)
    yield [own, other, own_far, dp_swap(other, 0)]


def scatter_halves(mine, theirs, order, hops):
    def added(first, second):
        return (first.astype(f32) + second.astype(f32)).astype(bf16)

    heard = dp_swap(theirs, 0)
    yield
    heard = order.next(heard)
    keep, other = added(mine[0], heard[0]), added(mine[1], heard[1])
    order.done(keep, other)
    heard = row_swap(other)
    yield
    total = added(keep, order.next(heard))
    order.done(total)
    if hops:
        size, col = lax.axis_size("col"), lax.axis_index("col")
        parts = jnp.stack([col_from(total[lax.rem(col + k, size)], k) for k in range(size)])
    else:
        parts = col_trade(total)
    yield
    total = jnp.sum(order.next(parts).astype(f32), 0)
    order.done(total)
    for bit in range(1, bits("dp")):
        total = total + dp_swap(total, bit)
    yield
    yield in_order(dp_bit(0), total, dp_swap(total, 0))


def after(value, *others):
    return lax.optimization_barrier((value, others))[0]


class Order:
    def __init__(self):
        self.last = ()

    def next(self, value):
        return after(value, self.last)

    def done(self, *results):
        self.last = results


def contract(first, second, first_axis, second_axis):
    return lax.dot_general(
        first, second, (((first_axis,), (second_axis,)), ((), ())), preferred_element_type=f32
    )


def turned(vectors):
    return vectors.astype(f32).T.astype(bf16)


def in_vmem(count):
    return [pl.BlockSpec(memory_space=pltpu.VMEM)] * count


def in_place(count):
    return [pl.BlockSpec(memory_space=pl.ANY)] * count


SCALARS = pl.BlockSpec(memory_space=pltpu.SMEM)


def like(shape, dtype):
    return jax.ShapeDtypeStruct(shape, dtype)


def cost(flops, moved, powers=0):
    return pl.CostEstimate(flops=flops, bytes_accessed=moved, transcendentals=powers)


def project_kernel(count, slots, scalars, h_ref, turn_ref, *refs):
    sources, w_ref, out_ref, sems = refs[:4], refs[4], refs[5], refs[6]
    part = sources[0].shape[2]
    rows = 3 * HALF
    copies = []
    for index, source in enumerate(sources):
        o, core = index % 2, index // 2
        place = scalars[2] ^ core
        for k in range(count):
            column = lax.rem(scalars[1] + count - k, count)
            for s in range(slots):
                start = pl.multiple_of(column * 3 * HEAD + place * rows, PAD)
                copies.append(
                    pltpu.make_async_copy(
                        source.at[k, pl.ds(s * rows, rows), :],
                        w_ref.at[s, pl.ds(start, rows), pl.ds(o * part, part)],
                        sems.at[len(copies)],
                    )
                )
    for copy in copies:
        copy.start()
    for copy in copies:
        copy.wait()
    h = h_ref[...]
    cosine, sine = turn_ref[0:HALF, :], turn_ref[HALF:HEAD, :]
    for s in range(slots):
        base = s * 3 * HEAD
        for k in range(count):
            values = contract(w_ref[s, k * 3 * HEAD : (k + 1) * 3 * HEAD, :], h, 1, 1)
            for i in range(2):
                low, middle, high = i * HEAD, i * HEAD + HALF, (i + 1) * HEAD
                first, second = values[low:middle], values[middle:high]
                out_ref[k, base + low : base + middle, :] = (first * cosine - second * sine).astype(bf16)
                out_ref[k, base + middle : base + high, :] = (second * cosine + first * sine).astype(bf16)
            out_ref[k, base + 2 * HEAD : base + 3 * HEAD, :] = values[2 * HEAD :].astype(bf16)


def project(scalars, h, turn, sources, slots):
    count, _, part = sources[0].shape
    width = h.shape[0]
    return pl.pallas_call(
        functools.partial(project_kernel, count, slots),
        in_specs=[SCALARS] + in_vmem(2) + in_place(len(sources)),
        out_specs=in_vmem(2),
        out_shape=[
            like((slots, count * 3 * HEAD, 2 * part), bf16),
            like((count, slots * 3 * HEAD, width), bf16),
        ],
        scratch_shapes=[pltpu.SemaphoreType.DMA((len(sources) * count * slots,))],
        cost_estimate=cost(slots * 2 * count * 3 * HEAD * 2 * part * width, 3_000_000 * slots),
        name="project",
    )(scalars, h, turn, *sources)


def pack_kernel(offset, _, own_ref, out_ref):
    for index in range(own_ref.shape[0]):
        out_ref[index] = own_ref[index, offset + HEAD : offset + 3 * HEAD, :]


def pack(scalars, own, offset):
    count, _, width = own.shape
    return pl.pallas_call(
        functools.partial(pack_kernel, offset),
        in_specs=[SCALARS] + in_vmem(1),
        out_specs=in_vmem(1)[0],
        out_shape=like((count, 2 * HEAD, width), bf16),
        cost_estimate=cost(1000, 1_000_000),
        name="pack",
    )(scalars, own)


def merge_kernel(_, d_query_ref, d_own_ref, heard_ref, out_ref):
    for index in range(out_ref.shape[0]):
        out_ref[index, :HEAD, :] = d_query_ref[index]
        out_ref[index, HEAD:, :] = (d_own_ref[index] + heard_ref[index].astype(f32)).astype(bf16)


def merge(scalars, d_query, d_own, heard):
    count, _, width = d_query.shape
    return pl.pallas_call(
        merge_kernel,
        in_specs=[SCALARS] + in_vmem(3),
        out_specs=in_vmem(1)[0],
        out_shape=like((count, 3 * HEAD, width), bf16),
        cost_estimate=cost(1000, 2_000_000),
        name="merge",
    )(scalars, d_query, d_own, heard)


def place_stripes(scalars, own_ref, offset, other_ref, keys, values_t, keys_t=None, values=None):
    side = scalars[2]
    count, _, width = own_ref.shape
    parts = width // LANES
    for place in range(count):
        for stripe, ref, base in (
            (2 * place + side, own_ref.at[place], offset + HEAD),
            (2 * place + 1 - side, other_ref.at[place], 0),
        ):
            start = pl.multiple_of(stripe * width, LANES)
            key_t = ref[base : base + HEAD, :]
            value_t = ref[base + HEAD : base + 2 * HEAD, :]
            keys[pl.ds(start, width), :] = turned(key_t)
            if values is not None:
                values[pl.ds(start, width), :] = turned(value_t)
            for part in range(parts):
                lanes = slice(part * LANES, (part + 1) * LANES)
                if values_t is not None:
                    values_t[stripe * parts + part] = value_t[:, lanes]
                if keys_t is not None:
                    keys_t[stripe * parts + part] = key_t[:, lanes]


def lane_block(ref, block):
    parts = KEYS // LANES
    return jnp.concatenate([ref[block * parts + part] for part in range(parts)], 1)


def attend_kernel(offset, earlier, scalars, own_ref, other_ref, limit_ref, *refs):
    before_ref, (out_ref, wide_ref, log_ref, keys, values_t) = refs[:earlier], refs[earlier:]
    count, _, width = own_ref.shape
    place_stripes(scalars, own_ref, offset, other_ref, keys, values_t)
    side = scalars[2]

    def stripe(place, _):
        query_t = own_ref[place, offset : offset + HEAD, :]
        limit = limit_ref[place]
        first = (2 * place + side) * width

        def step(masked, block, carry):
            top, total, mixed = carry
            start = pl.multiple_of(block * KEYS, KEYS)
            scores = jnp.dot(keys[pl.ds(start, KEYS), :], query_t, preferred_element_type=f32) * SCORE
            if masked:
                key = start + lax.broadcasted_iota(jnp.int32, scores.shape, 0)
                scores = jnp.where(key <= limit, scores, MASKED)
            new_top = jnp.maximum(top, jnp.max(scores, 0, keepdims=True))
            fade = jnp.exp2(top - new_top)
            weight = jnp.exp2(scores - new_top)
            total = total * fade + jnp.sum(weight, 0, keepdims=True)
            mixed = mixed * fade + jnp.dot(
                lane_block(values_t, block), weight.astype(bf16), preferred_element_type=f32
            )
            return new_top, total, mixed

        carry = (
            jnp.full((1, width), MASKED, f32),
            jnp.zeros((1, width), f32),
            jnp.zeros((HEAD, width), f32),
        )
        whole = first // KEYS
        carry = lax.fori_loop(0, whole, functools.partial(step, False), carry)
        top, total, mixed = lax.fori_loop(whole, scalars[3 + place], functools.partial(step, True), carry)
        mixed = mixed / total
        wide_ref[place] = mixed
        log_ref[place] = top + jnp.log2(total)
        return 0

    lax.fori_loop(0, count, stripe, 0)
    rows = out_ref.shape[1]
    for place in range(count):
        out_ref[place, rows - HEAD :, :] = wide_ref[place].astype(bf16)
        if earlier:
            out_ref[place, : rows - HEAD, :] = before_ref[0][place]


def attend(scalars, own, offset, other, limit, earlier):
    count, _, width = own.shape
    seq_len = 2 * count * width
    rows = HEAD + (earlier[0].shape[1] if earlier else 0)
    return pl.pallas_call(
        functools.partial(attend_kernel, offset, len(earlier)),
        in_specs=[SCALARS] + in_vmem(3 + len(earlier)),
        out_specs=in_vmem(3),
        out_shape=[
            like((count, rows, width), bf16),
            like((count, HEAD, width), f32),
            like((count, 1, width), f32),
        ],
        scratch_shapes=[
            pltpu.VMEM((seq_len, HEAD), bf16),
            pltpu.VMEM((seq_len // LANES, HEAD, LANES), bf16),
        ],
        cost_estimate=cost(8_000_000_000, 3_000_000, 3_000_000),
        name="attend",
    )(scalars, own, other, limit, *earlier)


def attend_back_kernel(
    offset,
    grad_offset,
    scalars,
    own_ref,
    other_ref,
    grad_ref,
    wide_ref,
    log_ref,
    limit_ref,
    turn_ref,
    d_query_ref,
    d_own_ref,
    d_other_ref,
    keys,
    values,
    keys_t,
    d_keys,
    d_values,
):
    count, _, width = own_ref.shape
    place_stripes(scalars, own_ref, offset, other_ref, keys, None, keys_t, values)
    side = scalars[2]
    d_keys[...] = jnp.zeros_like(d_keys)
    d_values[...] = jnp.zeros_like(d_values)

    def turn_back(vectors, stripe):
        cosine, sine = turn_ref[stripe, 0:HALF, :], turn_ref[stripe, HALF:HEAD, :]
        upper, lower = vectors[0:HALF], vectors[HALF:HEAD]
        return jnp.concatenate([upper * cosine + lower * sine, lower * cosine - upper * sine], 0)

    def of_stripe(place, _):
        query_t = own_ref[place, offset : offset + HEAD, :]
        grad_t = grad_ref[place, grad_offset : grad_offset + HEAD, :]
        query = turned(query_t)
        grad = turned(grad_t)
        drift = jnp.sum(grad_t.astype(f32) * wide_ref[place], 0, keepdims=True)
        log_sum = log_ref[place]
        limit = limit_ref[place]
        stripe = 2 * place + side

        def step(masked, block, d_query):
            start = pl.multiple_of(block * KEYS, KEYS)
            rows = pl.ds(start, KEYS)
            scores = jnp.dot(keys[rows, :], query_t, preferred_element_type=f32) * SCORE
            weight = jnp.exp2(scores - log_sum)
            if masked:
                key = start + lax.broadcasted_iota(jnp.int32, scores.shape, 0)
                weight = jnp.where(key <= limit, weight, 0.0)
            d_weight = jnp.dot(values[rows, :], grad_t, preferred_element_type=f32)
            d_scores = (weight * (d_weight - drift)).astype(bf16)
            d_values[rows, :] += jnp.dot(weight.astype(bf16), grad, preferred_element_type=f32)
            d_keys[rows, :] += jnp.dot(d_scores, query, preferred_element_type=f32)
            return d_query + jnp.dot(lane_block(keys_t, block), d_scores, preferred_element_type=f32)

        d_query = jnp.zeros((HEAD, width), f32)
        whole = stripe * width // KEYS
        d_query = lax.fori_loop(0, whole, functools.partial(step, False), d_query)
        d_query = lax.fori_loop(whole, scalars[3 + place], functools.partial(step, True), d_query)
        d_query_ref[place] = turn_back(d_query * HEAD ** (-0.5), stripe).astype(bf16)
        return 0

    lax.fori_loop(0, count, of_stripe, 0)

    def finish(place, _):
        for stripe, ref in ((2 * place + side, d_own_ref), (2 * place + 1 - side, d_other_ref)):
            start = pl.multiple_of(stripe * width, LANES)
            d_key = d_keys[pl.ds(start, width), :].T * HEAD ** (-0.5)
            ref[place, 0:HEAD, :] = turn_back(d_key, stripe).astype(ref.dtype)
            ref[place, HEAD : 2 * HEAD, :] = d_values[pl.ds(start, width), :].T.astype(ref.dtype)
        return 0

    lax.fori_loop(0, count, finish, 0)


def attend_back(scalars, own, offset, other, grad, grad_offset, wide, log_sum, limit, turns):
    count, _, width = own.shape
    seq_len = 2 * count * width
    return pl.pallas_call(
        functools.partial(attend_back_kernel, offset, grad_offset),
        in_specs=[SCALARS] + in_vmem(7),
        out_specs=in_vmem(3),
        out_shape=[
            like((count, HEAD, width), bf16),
            like((count, 2 * HEAD, width), f32),
            like((count, 2 * HEAD, width), bf16),
        ],
        scratch_shapes=[
            pltpu.VMEM((seq_len, HEAD), bf16),
            pltpu.VMEM((seq_len, HEAD), bf16),
            pltpu.VMEM((seq_len // LANES, HEAD, LANES), bf16),
            pltpu.VMEM((seq_len, HEAD), f32),
            pltpu.VMEM((seq_len, HEAD), f32),
        ],
        cost_estimate=cost(16_000_000_000, 4_000_000, 3_000_000),
        name="attend_back",
    )(scalars, own, other, grad, wide, log_sum, limit, turns)


SMALL = 9
SHIFT_A, SCALE_A, GATE_A, SHIFT_M, SCALE_M, GATE_M, GAIN_A, GAIN_M, BIAS_DOWN = range(SMALL)


def middle_kernel(slots, scalars, x_own, x_other, g_own, g_other, small_ref, first_ref, last_ref, source, *refs):
    block_own, block_other, d_middle_ref, h_ref, df_ref, d_att_ref, active_ref, d_hidden_ref, mixed_ref, sums_ref = refs[:10]
    d_first, d_last, w_out, up, down, bias, attended_ref, mid_ref, f_ref, dh_ref, sems = refs[10:]
    width, part = x_own.shape
    count = first_ref.shape[0]
    out_rows = slots * HEAD // SLICES
    step_rows = part // 2
    copies = {"out": [], "up": [], "down": [], "bias": []}
    used = 0

    def copy(kind, origin, target):
        nonlocal used
        copies[kind].append(pltpu.make_async_copy(origin, target, sems.at[used]))
        used += 1

    for index in range(SLICES):
        y, core = index // 2, index % 2
        for o in range(2):
            lanes = pl.ds(o * part, part)
            for k in range(count):
                b = core * count + k
                origin = source.at[index, scalars[0] ^ o, k]
                start = k * slots * HEAD + (2 * core + y) * out_rows
                copy("out", origin.at[pl.ds(0, out_rows), :], w_out.at[pl.ds(start, out_rows), lanes])
                start = y * step_rows
                copy("down", origin.at[pl.ds(out_rows, step_rows), :], down.at[b, pl.ds(start, step_rows), lanes])
                copy(
                    "up",
                    origin.at[pl.ds(out_rows + step_rows, step_rows), :],
                    up.at[b, pl.ds(o * part + start, step_rows), :],
                )
                if o == 0 and y == 0:
                    copy("bias", origin.at[pl.ds(out_rows + 2 * step_rows, PAD), :], bias.at[b])
    for kind in copies:
        for each in copies[kind]:
            each.start()
    for k in range(count):
        base = k * slots * HEAD
        mixed_ref[base : base + (slots - 1) * HEAD, :] = first_ref[k]
        mixed_ref[base + (slots - 1) * HEAD : base + slots * HEAD, :] = last_ref[k]

    def small(index):
        return small_ref[index : index + 1, :]

    def wide_rows(own, other, rows):
        return jnp.concatenate([own[rows, :].astype(f32), other[rows, :].astype(f32)], 1)

    def norm(values, rows):
        mean = jnp.mean(values, 1, keepdims=True)
        centered = values - mean
        inv_std = lax.rsqrt(jnp.mean(centered * centered, 1, keepdims=True) + epsilon)
        return centered * inv_std, inv_std

    for each in copies["out"]:
        each.wait()
    attended_ref[...] = contract(mixed_ref[...], w_out[...], 0, 0)
    f_ref[...] = jnp.zeros_like(f_ref)
    dh_ref[...] = jnp.zeros_like(dh_ref)
    sums_ref[...] = jnp.zeros_like(sums_ref)

    def before(index, _):
        rows = pl.ds(pl.multiple_of(index * CHUNK, CHUNK), CHUNK)
        middle = wide_rows(x_own, x_other, rows) + small(GATE_A) * attended_ref[rows, :]
        mid_ref[rows, :] = middle
        normed, _ = norm(middle, rows)
        h_ref[rows, :] = (normed * (small(GAIN_M) * (1.0 + small(SCALE_M))) + small(SHIFT_M)).astype(bf16)
        df_ref[rows, :] = (wide_rows(g_own, g_other, rows) * small(GATE_M)).astype(bf16)
        return 0

    lax.fori_loop(0, width // CHUNK, before, 0)
    for kind in ("up", "down", "bias"):
        for each in copies[kind]:
            each.wait()

    def feed(b, _):
        h, df = h_ref[...], df_ref[...]
        u = contract(h, up[b], 1, 0) + bias[b][0:1, :].astype(f32)
        squared = u * u
        bent = jnp.tanh(0.79788456 * u * (1.0 + 0.044715 * squared))
        active = (0.5 * u * (1.0 + bent)).astype(bf16)
        slope = 0.5 * (1.0 + bent) + 0.5 * u * (1.0 - bent * bent) * (
            0.79788456 * (1.0 + 3.0 * 0.044715 * squared)
        )
        active_ref[b] = active
        d_hidden = (slope * contract(df, down[b], 1, 1)).astype(bf16)
        d_hidden_ref[b] = d_hidden
        f_ref[...] += contract(active, down[b], 1, 0)
        dh_ref[...] += contract(d_hidden, up[b], 1, 1)
        return 0

    lax.fori_loop(0, 2 * count, feed, 0)

    def after(index, _):
        rows = pl.ds(pl.multiple_of(index * CHUNK, CHUNK), CHUNK)
        middle = mid_ref[rows, :]
        branch = f_ref[rows, :] + small(BIAS_DOWN)
        out = (middle + small(GATE_M) * branch).astype(bf16)
        block_own[rows, :] = out[:, :part]
        block_other[rows, :] = out[:, part:]
        upstream = wide_rows(g_own, g_other, rows)
        normed, inv_std = norm(middle, rows)
        dh = dh_ref[rows, :]
        scaled = dh * (small(GAIN_M) * (1.0 + small(SCALE_M)))
        mean_grad = jnp.mean(scaled, 1, keepdims=True)
        mean_proj = jnp.mean(scaled * normed, 1, keepdims=True)
        d_middle = upstream + inv_std * (scaled - mean_grad - normed * mean_proj)
        d_middle_ref[rows, :] = d_middle
        d_att_ref[rows, :] = (d_middle * small(GATE_A)).astype(bf16)
        for i, value in enumerate(
            (d_middle * attended_ref[rows, :], dh, dh * normed, upstream * branch, df_ref[rows, :].astype(f32))
        ):
            sums_ref[i : i + 1, :] += jnp.sum(value, 0, keepdims=True)
        return 0

    lax.fori_loop(0, width // CHUNK, after, 0)
    d_att = d_att_ref[...]
    for k in range(count):
        base = k * slots * HEAD
        values = contract(w_out[base : base + slots * HEAD, :], d_att, 1, 1).astype(bf16)
        d_first[k] = values[: (slots - 1) * HEAD]
        d_last[k] = values[(slots - 1) * HEAD :]


def middle(scalars, x, g, small, first, last, source, slots):
    count = first.shape[0]
    width, part = x[0].shape
    blocks = 2 * count
    heads = count * slots * HEAD
    return pl.pallas_call(
        functools.partial(middle_kernel, slots),
        in_specs=[SCALARS] + in_vmem(7) + in_place(1),
        out_specs=in_vmem(12),
        out_shape=[
            like((width, part), bf16),
            like((width, part), bf16),
            like((width, 2 * part), f32),
            like((width, 2 * part), bf16),
            like((width, 2 * part), bf16),
            like((width, 2 * part), bf16),
            like((blocks, width, part), bf16),
            like((blocks, width, part), bf16),
            like((heads, width), bf16),
            like((8, 2 * part), f32),
            like((count, (slots - 1) * HEAD, width), bf16),
            like((count, HEAD, width), bf16),
        ],
        scratch_shapes=[
            pltpu.VMEM((heads, 2 * part), bf16),
            pltpu.VMEM((blocks, 2 * part, part), bf16),
            pltpu.VMEM((blocks, part, 2 * part), bf16),
            pltpu.VMEM((blocks, PAD, part), bf16),
            pltpu.VMEM((width, 2 * part), f32),
            pltpu.VMEM((width, 2 * part), f32),
            pltpu.VMEM((width, 2 * part), f32),
            pltpu.VMEM((width, 2 * part), f32),
            pltpu.SemaphoreType.DMA(((6 * SLICES + 2) * count,)),
        ],
        cost_estimate=cost(2 * width * (4 * blocks * part * 2 * part + 2 * heads * 2 * part), 14_000_000, 2_000_000),
        name="middle",
    )(scalars, *x, *g, small, first, last, source)


def grads_kernel(slots, scalars, h_ref, df_ref, d_att_ref, active_ref, d_hidden_ref, mixed_ref, out_ref, d_out):
    part = h_ref.shape[1] // 2
    count = active_ref.shape[0] // 2
    out_rows = slots * HEAD // SLICES
    step_rows = part // 2
    d_out[...] = contract(mixed_ref[...], d_att_ref[...], 1, 0).astype(bf16)

    def of_block(b, _):
        core, k = b // count, b % count
        d_hidden = d_hidden_ref[b]
        d_up = contract(h_ref[...], d_hidden, 0, 0).astype(bf16)
        d_down = contract(active_ref[b], df_ref[...], 0, 0).astype(bf16)
        d_bias = jnp.broadcast_to(jnp.sum(d_hidden.astype(f32), 0, keepdims=True), (PAD, part)).astype(bf16)
        for y in range(2):
            start = pl.multiple_of(k * slots * HEAD + (2 * core + y) * out_rows, PAD)
            out_part = d_out[pl.ds(start, out_rows), :]
            for o in range(2):
                target = out_ref.at[2 * y + core, scalars[0] ^ o, k]
                lanes = slice(o * part, (o + 1) * part)
                start = o * part + y * step_rows
                target[:out_rows, :] = out_part[:, lanes]
                target[out_rows : out_rows + step_rows, :] = d_down[y * step_rows : (y + 1) * step_rows, lanes]
                target[out_rows + step_rows : out_rows + 2 * step_rows, :] = d_up[start : start + step_rows]
                target[out_rows + 2 * step_rows :, :] = d_bias
        return 0

    lax.fori_loop(0, 2 * count, of_block, 0)


def weight_grads(scalars, h, df, d_att, active, d_hidden, mixed, slots):
    count = active.shape[0] // 2
    width, whole = h.shape
    part = whole // 2
    return pl.pallas_call(
        functools.partial(grads_kernel, slots),
        in_specs=[SCALARS] + in_vmem(6),
        out_specs=in_vmem(1)[0],
        out_shape=like((SLICES, 2, count, slots * HEAD // SLICES + part + PAD, part), bf16),
        scratch_shapes=[pltpu.VMEM((mixed.shape[0], whole), bf16)],
        cost_estimate=cost(2 * width * (4 * count * part * whole + mixed.shape[0] * whole), 20_000_000),
        name="weight_grads",
    )(scalars, h, df, d_att, active, d_hidden, mixed)


def unproject_kernel(scalars, h_ref, w_ref, *refs):
    slots = w_ref.shape[0]
    pieces, (dh_ref, mine, theirs, grad) = refs[:slots], refs[slots:]
    count, rows, width = pieces[0].shape
    part = h_ref.shape[1] // 2
    half = rows // 2
    dh = jnp.zeros(dh_ref.shape, f32)
    for s in range(slots):
        back = pieces[s][...].reshape(count * rows, width)
        dh = dh + contract(back, w_ref[s], 0, 0)
        grad[...] = contract(back, h_ref[...], 1, 0).astype(bf16)
        for core, target in enumerate((mine, theirs)):
            place = scalars[2] ^ core
            for k in range(count):
                start = pl.multiple_of(k * rows + place * half, PAD)
                values = grad[pl.ds(start, half), :]
                for o in range(2):
                    target[o, k, s * half : (s + 1) * half, :] = values[:, o * part : (o + 1) * part]
    dh_ref[...] = dh


def unproject(scalars, h, weight, pieces):
    width, whole = h.shape
    slots = len(pieces)
    count = pieces[0].shape[0]
    shape = like((2, count, slots * 3 * HALF, whole // 2), bf16)
    return pl.pallas_call(
        unproject_kernel,
        in_specs=[SCALARS] + in_vmem(2 + slots),
        out_specs=in_vmem(3),
        out_shape=[like((width, whole), f32), shape, shape],
        scratch_shapes=[pltpu.VMEM((weight.shape[1], whole), bf16)],
        cost_estimate=cost(slots * 4 * width * whole * weight.shape[1], 5_000_000 * slots),
        name="unproject",
    )(scalars, h, weight, *pieces)


def embed_time(time_step):
    half_size = COND // 2
    frequency = jnp.exp(-math.log(10000.0) * jnp.arange(half_size, dtype=f32) / half_size)
    angles = time_step * frequency
    return jax.nn.silu(jnp.concatenate([jnp.cos(angles), jnp.sin(angles)]))


def shards(
    tokens, cotangent, timestep, piece_starts, w_mod, b_mod, gain_attn, w_qkv, w_out, gain_mlp, w_up, b_up, w_down, b_down
):
    cols = lax.axis_size("col")
    row, col, core, far = lax.axis_index("row"), lax.axis_index("col"), dp_bit(0), dp_bit(1)
    block_rows, part = tokens.shape
    width = block_rows // 2
    slots = w_qkv.shape[0] // (3 * HEAD)

    def relative(heard):
        return in_order(core ^ row, *heard)

    def half_rows(block):
        return relative(pair_to(half_at(block, row, 0), half_at(block, 1 - row, 0)))

    x = half_rows(tokens)

    order = Order()

    w_parts = w_qkv.reshape(slots, 3 * HEAD, part)
    groups = [(0, 1), (1, slots)]
    blocks = [half_at(w_parts[low:high], core, 1).reshape(-1, part) for low, high in groups]

    def quarter_at(block):
        return half_at(half_at(block, core, 0), far, 0)

    bias = jnp.broadcast_to(half_at(b_up[None], core, 1), (PAD, part))
    rest = jnp.concatenate(
        [quarter_at(w_out), quarter_at(w_down), half_at(half_at(w_up, core, 1), far, 0), bias], 0
    )

    condition = embed_time(timestep[0].astype(f32))
    modulation = jnp.einsum("k,kjd->jd", condition, w_mod.astype(f32), precision=precise) + b_mod
    known = jnp.concatenate([condition, piece_starts[0].astype(f32)])
    known = jnp.pad(known, (0, part - known.shape[0]))
    small = jnp.concatenate([modulation, gain_attn[None], gain_mlp[None], b_down[None], known[None]], 0)
    small = jnp.concatenate(relative(pair_to(small, small)), 1)
    condition = small[SMALL, :COND]
    starts = small[SMALL, COND : COND + piece_starts.shape[1]].astype(jnp.int32)

    residual = jnp.concatenate(x, 1).astype(f32)
    centered = residual - jnp.mean(residual, -1, keepdims=True)
    inv_std = lax.rsqrt(jnp.mean(centered * centered, -1, keepdims=True) + epsilon)
    gain_one = small[GAIN_A] * (1.0 + small[SCALE_A])
    h_one = (centered * inv_std * gain_one + small[SHIFT_A]).astype(bf16)

    lane = jnp.arange(width, dtype=jnp.int32)
    frequency = jnp.exp(-math.log(10000.0) * jnp.arange(HALF, dtype=f32) / HALF)
    places = jnp.arange(2 * cols, dtype=jnp.int32)[:, None] * width + lane[None]
    angles = places.astype(f32)[:, None, :] * frequency[None, :, None]
    turns = jnp.concatenate([jnp.cos(angles), jnp.sin(angles)], 1)
    here = lax.dynamic_index_in_dim(turns, 2 * col + core, 0, keepdims=False)
    own_stripes = 2 * jnp.arange(cols, dtype=jnp.int32) + core
    own_places = own_stripes[:, None] * width + lane[None]
    inside = (own_places[..., None] >= starts) & (own_places[..., None] < starts + PIECE)
    limit = jnp.max(jnp.where(inside, starts + PIECE - 1, own_places[..., None]), -1)
    scalars = jnp.concatenate(
        [jnp.stack([row, col, core]), jnp.max(limit, 1) // KEYS + 1]
    ).astype(jnp.int32)
    limit = limit[:, None, :]

    soon = gather_halves(blocks[0], order)
    next(soon)
    next(soon)
    rest = lax.all_gather(order.next(rest), ("dp", "row", "col"), axis=0, tiled=False)
    rest = rest.reshape((-1, 2, cols) + rest.shape[1:])[:SLICES]
    order.done(*order.last, *x, small)
    late = gather_halves(order.next(blocks[1]), order)
    next(late)
    soon = next(soon)
    next(late)
    w_groups, own = [], []

    def begin(group, source):
        low, high = groups[group]
        weight, pieces = project(order.next(scalars), h_one, here, source, high - low)
        order.done(weight)
        w_groups.append(weight)
        pieces = col_trade(pieces)
        own.extend((pieces, 3 * HEAD * i) for i in range(high - low))

    begin(0, soon)
    begin(1, next(late))
    g = half_rows(after(cotangent, w_groups[0]))
    forward, other = [], [None] * slots
    earlier = ()

    def share(slot):
        packed = pack(order.next(scalars), *own[slot])
        order.done(packed)
        other[slot] = dp_swap(packed, 0)

    share(0)
    for slot in range(slots):
        results = attend(order.next(scalars), *own[slot], other[slot], limit, earlier if slot < slots - 1 else ())
        order.done(results[2], *(g if slot == 1 else ()))
        forward.append(results)
        if slot < slots - 1:
            earlier = (results[0],)
        if slot == 0:
            for later in range(1, slots):
                share(later)
    first = col_trade(forward[slots - 2][0])
    last = col_trade(after(forward[slots - 1][0], first))

    kept = middle(order.next(scalars), x, g, small, first, last, rest, slots)
    (
        block_own,
        block_other,
        d_middle,
        h_two,
        d_branch,
        d_attended,
        active,
        d_hidden,
        mixed,
        sums,
        d_first,
        d_last,
    ) = kept
    order.done(d_middle)

    def whole_rows(own_part, other_part):
        return jnp.concatenate(in_order(row, *pair_from(*in_order(core ^ row, own_part, other_part))), 0)

    d_last = col_trade(d_last)
    grads = weight_grads(order.next(scalars), h_two, d_branch, d_attended, active, d_hidden, mixed, slots)
    order.done(grads)
    grads = after(grads, d_last)
    extra = lax.axis_size("dp") - SLICES
    grads = jnp.pad(grads, ((0, extra),) + ((0, 0),) * 4) if extra else grads
    grads = lax.psum_scatter(
        grads.reshape((-1,) + grads.shape[3:]), ("dp", "row", "col"), scatter_dimension=0, tiled=True
    )
    d_first = col_trade(d_first)
    block_out = whole_rows(block_own, block_other)

    back, shared = {}, {}

    def pull(slot):
        grad = (d_last, 0) if slot == slots - 1 else (d_first, slot * HEAD)
        d_query, d_own, d_other = attend_back(
            order.next(scalars), *own[slot], other[slot], *grad, *forward[slot][1:], limit, turns
        )
        order.done(d_other, *((block_out,) if slot == slots - 2 else ()))
        shared[slot] = d_query, d_own, dp_swap(d_other, 0)

    def send(slot):
        pieces = merge(order.next(scalars), *shared[slot])
        order.done(pieces)
        back[slot] = col_trade(pieces)

    d_hs = []

    def finish(group):
        low, high = groups[group]
        pieces = [back[slot] for slot in range(low, high)]
        d_h, mine, theirs = unproject(order.next(scalars), h_one, w_groups[group], pieces)
        order.done(d_h)
        d_hs.append(d_h)
        steps = scatter_halves(mine, theirs, order, group > 0)
        next(steps)
        return steps

    for slot in reversed(range(slots)):
        pull(slot)
        if slot < slots - 1:
            send(slot + 1)
    send(0)
    late = finish(1)
    next(late)
    next(late)
    soon = finish(0)
    d_h_one = d_hs[0] + d_hs[1]
    normed = centered * inv_std
    scaled = d_h_one * gain_one
    mean_grad = jnp.mean(scaled, -1, keepdims=True)
    mean_proj = jnp.mean(scaled * normed, -1, keepdims=True)
    d_tokens = d_middle + inv_std * (scaled - mean_grad - normed * mean_proj)
    sums = jnp.concatenate([jnp.sum(d_h_one, 0)[None], jnp.sum(d_h_one * normed, 0)[None], sums[:5]], 0)

    order.done(d_tokens, sums)
    next(soon)
    tokens_out = whole_rows(d_tokens[:, :part], d_tokens[:, part:])

    sums = order.next(sums)
    sums = sums + dp_swap(sums, 0)
    for bit in range(bits("col")):
        sums = sums + col_swap(sums, bit)
        order.done(sums)
        if bit == 0:
            next(soon)
            next(late)
            sums = order.next(sums)
    per_seq = jnp.concatenate(
        [
            sums[0:1],
            sums[1:2] * small[GAIN_A],
            sums[2:4],
            sums[4:5] * small[GAIN_M],
            sums[5:6],
            sums[1:2] * (1.0 + small[SCALE_A]),
            sums[4:5] * (1.0 + small[SCALE_M]),
            sums[6:7],
            jnp.tile(jnp.pad(condition, (0, part - COND)), 2)[None],
        ],
        0,
    )[None]
    per_seq = jnp.concatenate(in_order(row, per_seq[..., :part], row_swap(per_seq[..., part:])), 0)
    order.done(per_seq)
    next(soon)
    for bit in range(1, bits("dp")):
        per_seq = jnp.concatenate(in_order(dp_bit(bit), per_seq, dp_swap(per_seq, bit)), 0)
    late, soon = next(late), next(soon)
    d_qkv = []
    for (low, high), found in zip(groups, (soon, late)):
        parts = [half.reshape(high - low, -1, part) for half in found]
        d_qkv.append(jnp.concatenate(parts, 1).reshape(-1, part))
    d_qkv = jnp.concatenate(d_qkv, 0)

    grads = lax.all_gather(grads[0], "dp", axis=0, tiled=False)[:SLICES].astype(f32)
    rows = slots * HEAD // SLICES
    step = part // 2
    ordered = [grads[2 * y + c] for c in range(2) for y in range(2)]
    d_out_proj = jnp.concatenate([each[:rows] for each in ordered], 0)
    d_down = jnp.concatenate([each[rows : rows + step] for each in ordered], 0)
    d_up = jnp.concatenate(
        [
            jnp.concatenate([grads[2 * y + c, rows + step : rows + 2 * step] for c in range(2)], 1)
            for y in range(2)
        ],
        0,
    )
    d_bias = jnp.concatenate([grads[c, rows + 2 * step] for c in range(2)], 0)

    conditions = per_seq[:, SMALL, :COND]
    d_mod_w = sum(conditions[s][:, None, None] * per_seq[s, :6][None] for s in range(per_seq.shape[0]))
    totals = jnp.sum(per_seq[:, :SMALL], 0)

    return (
        block_out,
        tokens_out,
        d_mod_w,
        totals[:6],
        totals[6],
        d_qkv,
        d_out_proj,
        totals[7],
        d_up,
        d_bias,
        d_down,
        totals[8],
    )


def solution(mesh):
    blocks = P(("dp", "col"), "row")
    return jax.shard_map(
        shards,
        mesh=mesh,
        in_specs=(
            blocks,
            blocks,
            P("dp"),
            P("dp", None),
            P(None, None, "row"),
            P(None, "row"),
            P("row"),
            P("col", "row"),
            P("col", "row"),
            P("row"),
            P("row", "col"),
            P("col"),
            P("col", "row"),
            P("row"),
        ),
        out_specs=(
            blocks,
            blocks,
            P(None, None, "row"),
            P(None, "row"),
            P("row"),
            P("col", "row"),
            P("col", "row"),
            P("row"),
            P("row", "col"),
            P("col"),
            P("col", "row"),
            P("row"),
        ),
        check_vma=False,
    )
```
